128 devices in a mesh: band: 64 (over z, y, x), head: 2 (over core).
Axes of the slice: x: 4, y: 4, z: 4, core: 2. Of those that a mesh axis runs over, the one named last changes fastest.
Arguments:
- grid_state: bfloat16 [262144, 100], P('band'), may hold values from -6 to 6
- hidden_state: bfloat16 [65536, 1024], P('band', 'head'), may hold values from -6 to 6
- encoder_sources: int32 [65536, 32], P('band'), may hold values from 0 to 12287, as said below
- encoder_counts: int32 [65536], P('band'), may hold values from 1 to 32
- decoder_sources: int32 [262144, 4], P('band'), may hold values from 0 to 65535, as said below
- decoder_counts: int32 [262144], P('band'), may hold values from 1 to 4
- encoder_keys: bfloat16 [100, 1024], P(None, 'head'), may hold values from -0.625 to 0.625
- encoder_values: bfloat16 [100, 1024], P(None, 'head'), may hold values from -0.625 to 0.625
- encoder_query: bfloat16 [1024, 1024], P(None, 'head'), may hold values from -0.1875 to 0.1875
- encoder_output: bfloat16 [1024, 1024], P('head'), may hold values from -0.1875 to 0.1875
- window_query: bfloat16 [1024, 1024], P(None, 'head'), may hold values from -0.1875 to 0.1875
- window_keys: bfloat16 [1024, 1024], P(None, 'head'), may hold values from -0.1875 to 0.1875
- window_values: bfloat16 [1024, 1024], P(None, 'head'), may hold values from -0.1875 to 0.1875
- window_output: bfloat16 [1024, 1024], P('head'), may hold values from -0.1875 to 0.1875
- feed_up: bfloat16 [1024, 4096], P(None, 'head'), may hold values from -0.1875 to 0.1875
- feed_down: bfloat16 [4096, 1024], P('head'), may hold values from -0.09375 to 0.09375
- decoder_query: bfloat16 [100, 1024], P(None, 'head'), may hold values from -0.625 to 0.625
- decoder_keys: bfloat16 [1024, 1024], P(None, 'head'), may hold values from -0.1875 to 0.1875
- decoder_values: bfloat16 [1024, 1024], P(None, 'head'), may hold values from -0.1875 to 0.1875
- decoder_output: bfloat16 [1024, 100], P('head'), may hold values from -0.1875 to 0.1875
Outputs:
- grid_next: bfloat16 [262144, 100], P(('band', 'head'))
- hidden_final: bfloat16 [65536, 1024], P('band', 'head')
The draws below stay inside these ranges and needn't reach their ends.
Inputs may be any that keep to these rules, and one draw needn't show every extreme that they name: Grid band c holds the grid points c * 4096 to (c + 1) * 4096 - 1 and hidden band c the hidden nodes c * 1024 to (c + 1) * 1024 - 1; slot e of hidden node n names the grid point (n // 1024 - 1) * 4096 + encoder_sources[n, e], which lies in a band that exists. Only the first encoder_counts[n] slots are edges. `decoder_sources`: every slot of grid point g names a hidden node of the bands g // 4096 - 1 to g // 4096 + 1 that exist. Only the first decoder_counts[g] slots are edges.
All inputs are finite; a program needn't handle non-finite values.
Results may differ from the reference program's by a relative error of at most 0.015.
Values may be sent and summed in bfloat16 or wider, within the bound.
A program may use at most 320 MiB of HBM per device.

```python
import jax
import jax.numpy as jnp
from jax import lax

D = 1024
FFN = 4096
VARS = 100
HALF_WIN = 560
H_DEV = 1024
G_DEV = 4096
E_ENC = 32
E_DEC = 4
HEAD_DIM = 64
HIDDEN_SIZE = 65536
GRID = 262144
N_BAND = 64
N_HEAD = 2


def draw_encoder_sources(key, part):
    target_band = jnp.arange(HIDDEN_SIZE, dtype=jnp.int32) // H_DEV
    lowest = jnp.where(target_band == 0, G_DEV, 0).astype(jnp.int32)
    highest = jnp.where(target_band == N_BAND - 1, 2 * G_DEV, 3 * G_DEV).astype(jnp.int32)
    return jax.random.randint(jax.random.fold_in(key, 11), (HIDDEN_SIZE, E_ENC), lowest[:, None], highest[:, None], dtype=jnp.int32)


def draw_decoder_sources(key, part):
    target_band = jnp.arange(GRID, dtype=jnp.int32) // G_DEV
    lowest = jnp.maximum(target_band - 1, 0) * H_DEV
    highest = jnp.minimum((target_band + 2) * H_DEV, HIDDEN_SIZE)
    return jax.random.randint(jax.random.fold_in(key, 23), (GRID, E_DEC), lowest[:, None], highest[:, None], dtype=jnp.int32)


def touch_ends(entries, rng, least, high):
    spot = [jax.random.randint(jax.random.fold_in(rng, axis), (), 0, length) for axis, length in enumerate(entries.shape)]
    widest = entries.shape.index(max(entries.shape))
    neighbour = spot[:widest] + [(spot[widest] + 1) % entries.shape[widest]] + spot[widest + 1:]
    return entries.at[tuple(spot)].set(least).at[tuple(neighbour)].set(high)


def steps_of(stream_key, shape, shards, least, top_value):
    def one(dim, parts):
        steps = jax.random.uniform(jax.random.fold_in(jax.random.fold_in(stream_key, 6), dim), (parts,), jnp.float32, least / len(shards), top_value / len(shards))
        return jnp.repeat(jnp.exp(steps), shape[dim] // parts).reshape((-1,) + (1,) * (len(shape) - dim - 1))

    loudness = one(*shards[0])
    for cut in shards[1:]:
        loudness = loudness * one(*cut)
    return loudness


def normal_values(key, extent, width, reach, pieces=(), kind=jnp.bfloat16):
    drawn = jax.random.normal(key, extent, jnp.float32) * width
    if len(pieces) > 0:
        drawn = steps_of(key, extent, pieces, -0.22, 0.18) * drawn
    return jnp.clip(drawn, min=-reach, max=reach).astype(kind)


def setup_inputs(seed: int = 0) -> dict:
    key_list = jax.random.split(jax.random.key(seed), 21)
    return {
        "grid_state": normal_values(key_list[0], (GRID, VARS), 1.0, 6.0, ((0, 64),)),
        "hidden_state": normal_values(key_list[1], (HIDDEN_SIZE, D), 1.0, 6.0, ((0, 64), (1, 2))),
        "encoder_sources": draw_encoder_sources(jax.random.fold_in(key_list[20], 71), 0),
        "encoder_counts": touch_ends(jax.random.randint(key_list[3], (HIDDEN_SIZE,), 1, E_ENC + 1), jax.random.fold_in(key_list[3], 1), 1, E_ENC).astype(jnp.int32),
        "decoder_sources": draw_decoder_sources(jax.random.fold_in(key_list[20], 71), 0),
        "decoder_counts": touch_ends(jax.random.randint(key_list[5], (GRID,), 1, E_DEC + 1), jax.random.fold_in(key_list[5], 1), 1, E_DEC).astype(jnp.int32),
        "encoder_keys": normal_values(key_list[6], (VARS, D), VARS ** -0.5, 0.625, ((1, 2),)),
        "encoder_values": normal_values(key_list[7], (VARS, D), VARS ** -0.5, 0.625, ((1, 2),)),
        "encoder_query": normal_values(key_list[8], (D, D), D ** -0.5, 0.1875, ((1, 2),)),
        "encoder_output": normal_values(key_list[9], (D, D), D ** -0.5, 0.1875, ((0, 2),)),
        "window_query": normal_values(key_list[10], (D, D), D ** -0.5, 0.1875, ((1, 2),)),
        "window_keys": normal_values(key_list[11], (D, D), D ** -0.5, 0.1875, ((1, 2),)),
        "window_values": normal_values(key_list[12], (D, D), D ** -0.5, 0.1875, ((1, 2),)),
        "window_output": normal_values(key_list[13], (D, D), D ** -0.5, 0.1875, ((0, 2),)),
        "feed_up": normal_values(key_list[14], (D, FFN), D ** -0.5, 0.1875, ((1, 2),)),
        "feed_down": normal_values(key_list[15], (FFN, D), FFN ** -0.5, 0.09375, ((0, 2),)),
        "decoder_query": normal_values(key_list[16], (VARS, D), VARS ** -0.5, 0.625, ((1, 2),)),
        "decoder_keys": normal_values(key_list[17], (D, D), D ** -0.5, 0.1875, ((1, 2),)),
        "decoder_values": normal_values(key_list[18], (D, D), D ** -0.5, 0.1875, ((1, 2),)),
        "decoder_output": normal_values(key_list[19], (D, VARS), D ** -0.5, 0.1875, ((0, 2),)),
    }


EPSILON = 1e-05
NEGATIVE = -1e+30

def layer_norm(matrix):
    as_float = matrix.astype(jnp.float32)
    centred = as_float - lax.optimization_barrier(jnp.mean(as_float, axis=-1, keepdims=True))
    variance = lax.optimization_barrier(jnp.mean(centred * centred, axis=-1, keepdims=True))
    return (centred * lax.rsqrt(variance + EPSILON)).astype(jnp.bfloat16)

def project(matrix, weight):
    return jnp.dot(matrix, weight, preferred_element_type=jnp.float32).astype(jnp.bfloat16)

def softmax_weights(scores):
    powers = jnp.exp(scores)
    return (powers / lax.optimization_barrier(jnp.sum(powers, axis=-1, keepdims=True))).astype(jnp.bfloat16)

def edge_attention(query, keys, values, counts):
    row_count, slot_count, full_width = keys.shape
    head_count = full_width // HEAD_DIM
    query_heads = query.reshape(row_count, head_count, HEAD_DIM).astype(jnp.float32)
    key_heads = keys.reshape(row_count, slot_count, head_count, HEAD_DIM).astype(jnp.float32)
    value_heads = values.reshape(row_count, slot_count, head_count, HEAD_DIM).astype(jnp.float32)
    scores = jnp.einsum('rhd,rehd->rhe', query_heads, key_heads) * HEAD_DIM ** (-0.5)
    slot_live = jnp.arange(slot_count, dtype=jnp.int32)[None, None, :] < counts.astype(jnp.int32)[:, None, None]
    weights = softmax_weights(jnp.where(slot_live, scores, NEGATIVE))
    mixed = jnp.einsum('rhe,rehd->rhd', weights.astype(jnp.float32), value_heads)
    return mixed.reshape(row_count, full_width).astype(jnp.bfloat16)

def window_attention(query, keys, values, live):
    query_count, full_width = query.shape
    span_count = keys.shape[0]
    head_count = full_width // HEAD_DIM
    query_heads = query.reshape(query_count, head_count, HEAD_DIM).astype(jnp.float32)
    key_heads = keys.reshape(span_count, head_count, HEAD_DIM).astype(jnp.float32)
    value_heads = values.reshape(span_count, head_count, HEAD_DIM).astype(jnp.float32)
    scores = jnp.einsum('qhd,shd->hqs', query_heads, key_heads) * HEAD_DIM ** (-0.5)
    weights = softmax_weights(jnp.where(live[None], scores, NEGATIVE))
    mixed = jnp.einsum('hqs,shd->qhd', weights.astype(jnp.float32), value_heads)
    return mixed.reshape(query_count, full_width).astype(jnp.bfloat16)

def head_sum(mixed, weight):
    row_count = mixed.shape[0]
    group_width = mixed.shape[1] // N_HEAD
    left_side = mixed.reshape(row_count, N_HEAD, group_width).astype(jnp.float32)
    right_side = weight.reshape(N_HEAD, group_width, weight.shape[1]).astype(jnp.float32)
    partials = jnp.einsum('rgc,gcd->rgd', left_side, right_side).astype(jnp.bfloat16)
    return lax.optimization_barrier(jnp.sum(partials.astype(jnp.float32), axis=1))

def reference(grid_state, hidden_state, encoder_sources, encoder_counts, decoder_sources, decoder_counts, encoder_keys, encoder_values, encoder_query, encoder_output, window_query, window_keys, window_values, window_output, feed_up, feed_down, decoder_query, decoder_keys, decoder_values, decoder_output):
    grid_key = project(grid_state, encoder_keys)
    grid_value = project(grid_state, encoder_values)
    enc_query = project(layer_norm(hidden_state), encoder_query)
    node_band = (jnp.arange(HIDDEN_SIZE, dtype=jnp.int32) // H_DEV).astype(jnp.int32)
    band_base = ((node_band - 1) * G_DEV).astype(jnp.int32)
    encoder_global = (encoder_sources.astype(jnp.int32) + band_base[:, None]).astype(jnp.int32)

    def encode(item):
        block_query, block_sources, block_counts = item
        return edge_attention(block_query, jnp.take(grid_key, block_sources, axis=0), jnp.take(grid_value, block_sources, axis=0), block_counts)
    enc_mix = lax.map(encode, (enc_query.reshape(N_BAND, H_DEV, D), encoder_global.reshape(N_BAND, H_DEV, E_ENC), encoder_counts.reshape(N_BAND, H_DEV))).reshape(HIDDEN_SIZE, D)
    hidden_mid = (hidden_state.astype(jnp.float32) + head_sum(enc_mix, encoder_output)).astype(jnp.bfloat16)
    normed_mid = layer_norm(hidden_mid)
    win_query = project(normed_mid, window_query)
    win_key = project(normed_mid, window_keys)
    win_value = project(normed_mid, window_values)
    padded_key = jnp.pad(win_key, ((HALF_WIN, HALF_WIN), (0, 0)))
    padded_value = jnp.pad(win_value, ((HALF_WIN, HALF_WIN), (0, 0)))
    block_rows = min(512, H_DEV)
    span_rows = block_rows + 2 * HALF_WIN

    def attend(start):
        block_query = lax.dynamic_slice_in_dim(win_query, start, block_rows, 0)
        block_key = lax.dynamic_slice_in_dim(padded_key, start, span_rows, 0)
        block_value = lax.dynamic_slice_in_dim(padded_value, start, span_rows, 0)
        query_pos = start + jnp.arange(block_rows, dtype=jnp.int32)
        key_pos = start - HALF_WIN + jnp.arange(span_rows, dtype=jnp.int32)
        distance = jnp.abs(query_pos[:, None] - key_pos[None, :])
        live = (distance <= HALF_WIN) & (key_pos[None, :] >= 0) & (key_pos[None, :] < HIDDEN_SIZE)
        return window_attention(block_query, block_key, block_value, live)
    starts = (jnp.arange(HIDDEN_SIZE // block_rows, dtype=jnp.int32) * block_rows).astype(jnp.int32)
    win_mix = lax.map(attend, starts).reshape(HIDDEN_SIZE, D)
    hidden_att = (hidden_mid.astype(jnp.float32) + head_sum(win_mix, window_output)).astype(jnp.bfloat16)
    inner = jax.nn.gelu(jnp.dot(layer_norm(hidden_att), feed_up, preferred_element_type=jnp.float32), approximate=True).astype(jnp.bfloat16)
    hidden_final = (hidden_att.astype(jnp.float32) + head_sum(inner, feed_down)).astype(jnp.bfloat16)
    normed_final = layer_norm(hidden_final)
    dec_key = project(normed_final, decoder_keys)
    dec_value = project(normed_final, decoder_values)
    dec_query = project(grid_state, decoder_query)

    def decode(item):
        block_query, block_sources, block_counts = item
        return edge_attention(block_query, jnp.take(dec_key, block_sources, axis=0), jnp.take(dec_value, block_sources, axis=0), block_counts)
    dec_mix = lax.map(decode, (dec_query.reshape(N_BAND, G_DEV, D), decoder_sources.reshape(N_BAND, G_DEV, E_DEC), decoder_counts.reshape(N_BAND, G_DEV))).reshape(GRID, D)
    update = jnp.dot(dec_mix, decoder_output, preferred_element_type=jnp.float32)
    grid_next = (grid_state.astype(jnp.float32) + update).astype(jnp.bfloat16)
    return (grid_next, hidden_final)
```

```python
import functools

import jax
import jax.numpy as jnp
from jax import lax
from jax.experimental import pallas as pl
from jax.experimental.pallas import tpu as pltpu
from jax.sharding import PartitionSpec as P

HALF_WIN = 560
HEAD_DIM = 64
EPSILON = 1e-05
NEGATIVE = -1e30
SCALE = HEAD_DIM**-0.5
MESH = pl.DeviceIdType.MESH
NB = 16
QB = 128
GB = 64
RB = 256
ANY = pl.BlockSpec(memory_space=pl.ANY)
VM = pl.BlockSpec(memory_space=pltpu.VMEM)


def layer_norm(matrix):
    as_float = matrix.astype(jnp.float32)
    centred = as_float - jnp.mean(as_float, axis=-1, keepdims=True)
    variance = jnp.mean(centred * centred, axis=-1, keepdims=True)
    return (centred * lax.rsqrt(variance + EPSILON)).astype(jnp.bfloat16)


def project(matrix, weight):
    return jnp.dot(matrix, weight, preferred_element_type=jnp.float32).astype(jnp.bfloat16)


def places():
    band = lax.axis_index("band")
    head = lax.axis_index("head")
    count = lax.axis_size("band")
    left = lax.rem(band + count - 1, count)
    right = lax.rem(band + 1, count)
    return band, head, left, right


def greet(others):
    barrier = pltpu.get_barrier_semaphore()
    for other in others:
        pl.semaphore_signal(barrier, inc=1, device_id=other, device_id_type=MESH)
    pl.semaphore_wait(barrier, len(others))


class Sender:
    def __init__(self, send_sem, recv_sem):
        self.send_sem, self.recv_sem, self.used, self.open = send_sem, recv_sem, 0, []

    def send(self, src, dst, device):
        n = self.used
        self.used += 1
        copy = pltpu.make_async_remote_copy(
            src_ref=src, dst_ref=dst, send_sem=self.send_sem.at[n], recv_sem=self.recv_sem.at[n],
            device_id=device, device_id_type=MESH)
        copy.start()
        self.open.append(copy)
        return copy

    def finish(self, received=()):
        for copy in self.open:
            copy.wait_send()
            if not any(copy is other for other in received):
                copy.wait_recv()


def half_of(ref, dim, index):
    size = ref.shape[dim] // 2
    part = pl.ds(pl.multiple_of(index * size, size), size)
    return ref.at[part] if dim == 0 else ref.at[:, part]


def relay(near, source, width, sides, sender, me, band, left, right, head, chunks):
    step = width // 2 // chunks
    waves = []
    for c in range(chunks):
        own = pl.ds(pl.multiple_of(head * (width // 2) + c * step, step), step)
        for side, other in ((sides[0], right), (sides[1], left)):
            rows = pl.ds(pl.multiple_of(side * width + head * (width // 2) + c * step, step), step)
            waves.append((sender.send(source(own, c, step), near.at[rows], (other, head)), rows))
    return waves


def start_kernel(n_pair, dims, *refs):
    grid, state = refs[0], refs[1]
    halves = refs[2 : 2 + n_pair]
    near, whole = refs[2 + n_pair], refs[3 + n_pair]
    fulls = refs[4 + n_pair : 4 + 2 * n_pair]
    rest = refs[4 + 2 * n_pair :]
    state_hold = rest[0]
    holds = rest[1 : 1 + n_pair]
    send_sem, recv_sem, load_sem, store_sem = rest[1 + n_pair :]
    band, head, left, right = places()
    peer = (band, 1 - head)
    loads = [pltpu.make_async_copy(half_of(state, 0, head), state_hold, load_sem.at[n_pair])]
    loads += [pltpu.make_async_copy(h, v, load_sem.at[n]) for n, (h, v) in enumerate(zip(halves, holds))]
    for load in loads:
        load.start()
    greet([peer, (left, head), (right, head)])
    sender = Sender(send_sem, recv_sem)
    waves = relay(near, lambda own, c, step: grid.at[own], grid.shape[0], (0, 1), sender, None, band, left, right, head, 4)
    sender.send(half_of(state, 0, 1 - head), half_of(whole, 1, head), peer)
    for n in range(n_pair):
        sender.send(halves[n], half_of(fulls[n], dims[n], head), peer)
    stores = [pltpu.make_async_copy(state_hold, half_of(whole, 1, head), store_sem.at[n_pair])]
    stores += [pltpu.make_async_copy(holds[n], half_of(fulls[n], dims[n], head), store_sem.at[n]) for n in range(n_pair)]
    for load, store in zip(loads, stores):
        load.wait()
        store.start()
    for copy, rows in waves:
        copy.wait_recv()
        sender.send(near.at[rows], near.at[rows], peer)
    sender.finish([copy for copy, _ in waves])
    for store in stores:
        store.wait()


def full_shape(half, dim):
    shape = list(half.shape)
    shape[dim] *= 2
    return jax.ShapeDtypeStruct(tuple(shape), half.dtype)


def start_exchange(grid, state, pairs):
    halves = [half for half, _ in pairs]
    dims = [dim for _, dim in pairs]
    n = len(pairs)
    nodes, width = state.shape
    outs = [jax.ShapeDtypeStruct((2 * grid.shape[0], grid.shape[1]), grid.dtype),
            jax.ShapeDtypeStruct((nodes // 2, width * 2), state.dtype)]
    outs += [full_shape(half, dim) for half, dim in pairs]
    copies = 16 + 1 + n
    return pl.pallas_call(
        functools.partial(start_kernel, n, dims),
        out_shape=outs,
        in_specs=[VM] + [ANY] * (n + 1),
        out_specs=[ANY] * (n + 2),
        scratch_shapes=[pltpu.VMEM((nodes // 2, width), state.dtype)]
        + [pltpu.VMEM(half.shape, half.dtype) for half in halves]
        + [pltpu.SemaphoreType.DMA((copies,))] * 2
        + [pltpu.SemaphoreType.DMA((n + 1,))] * 2,
        compiler_params=pltpu.CompilerParams(collective_id=0, has_side_effects=True, vmem_limit_bytes=32 << 20),
        name="start_exchange",
    )(grid, state, *halves)


def window_kernel_exchange(n_pair, dims, *refs):
    rows = refs[0]
    halves = refs[1 : 1 + n_pair]
    span = refs[1 + n_pair]
    fulls = refs[2 + n_pair : 2 + 2 * n_pair]
    rest = refs[2 + 2 * n_pair :]
    holds = rest[:n_pair]
    send_sem, recv_sem, load_sem, store_sem = rest[n_pair:]
    band, head, left, right = places()
    count = rows.shape[0]
    extra = HALF_WIN - count
    after = HALF_WIN + count
    peer = (band, 1 - head)
    across = (lax.rem(band + lax.axis_size("band") + 2 * head - 1, lax.axis_size("band")), 1 - head)
    loads = [pltpu.make_async_copy(h, v, load_sem.at[n]) for n, (h, v) in enumerate(zip(halves, holds))]
    for load in loads:
        load.start()
    own = pltpu.make_async_copy(rows, span.at[pl.ds(HALF_WIN, count)], store_sem.at[n_pair])
    own.start()
    greet([peer, (left, head), (right, head), across])
    sender = Sender(send_sem, recv_sem)
    sender.send(rows, span.at[pl.ds(pl.multiple_of(after + head * (extra - after), 16), count)], across)
    sender.send(rows.at[pl.ds(count - extra, extra)], span.at[pl.ds(0, extra)], (right, head))
    sender.send(rows.at[pl.ds(0, extra)], span.at[pl.ds(after + count, extra)], (left, head))
    sender.send(rows, span.at[pl.ds(pl.multiple_of(extra + head * (after - extra), 16), count)], peer)
    for n in range(n_pair):
        sender.send(halves[n], half_of(fulls[n], dims[n], head), peer)
    stores = [pltpu.make_async_copy(holds[n], half_of(fulls[n], dims[n], head), store_sem.at[n]) for n in range(n_pair)]
    for load, store in zip(loads, stores):
        load.wait()
        store.start()
    sender.finish()
    own.wait()
    for store in stores:
        store.wait()


def window_exchange(rows, span_rows, pairs):
    halves = [half for half, _ in pairs]
    dims = [dim for _, dim in pairs]
    n = len(pairs)
    outs = [jax.ShapeDtypeStruct((span_rows, rows.shape[1]), rows.dtype)]
    outs += [full_shape(half, dim) for half, dim in pairs]
    copies = 4 + n
    return pl.pallas_call(
        functools.partial(window_kernel_exchange, n, dims),
        out_shape=outs,
        in_specs=[VM] + [ANY] * n,
        out_specs=[ANY] * (n + 1),
        scratch_shapes=[pltpu.VMEM(half.shape, half.dtype) for half in halves]
        + [pltpu.SemaphoreType.DMA((copies,))] * 2
        + [pltpu.SemaphoreType.DMA((n + 1,))] * 2,
        compiler_params=pltpu.CompilerParams(collective_id=1, has_side_effects=True, vmem_limit_bytes=32 << 20),
        name="window_exchange",
    )(rows, *halves)


def final_kernel_exchange(n_pair, dims, *refs):
    rows = refs[0]
    halves = refs[1 : 1 + n_pair]
    near = refs[1 + n_pair]
    fulls = refs[2 + n_pair : 2 + 2 * n_pair]
    rest = refs[2 + 2 * n_pair :]
    holds = rest[:n_pair]
    send_sem, recv_sem, load_sem, store_sem = rest[n_pair:]
    band, head, left, right = places()
    count = rows.shape[0]
    peer = (band, 1 - head)
    loads = [pltpu.make_async_copy(h, v, load_sem.at[n]) for n, (h, v) in enumerate(zip(halves, holds))]
    for load in loads:
        load.start()
    mine = pl.ds(pl.multiple_of(2 * count + head * count, count), count)
    own = pltpu.make_async_copy(rows, near.at[mine], store_sem.at[n_pair])
    own.start()
    greet([peer, (left, head), (right, head)])
    sender = Sender(send_sem, recv_sem)
    waves = relay(near, lambda o, c, step: rows.at[pl.ds(c * step, step)], 2 * count, (0, 2), sender, None, band, left, right, head, 4)
    sender.send(rows, near.at[mine], peer)
    for n in range(n_pair):
        sender.send(halves[n], half_of(fulls[n], dims[n], head), peer)
    stores = [pltpu.make_async_copy(holds[n], half_of(fulls[n], dims[n], head), store_sem.at[n]) for n in range(n_pair)]
    for load, store in zip(loads, stores):
        load.wait()
        store.start()
    for copy, place in waves:
        copy.wait_recv()
        sender.send(near.at[place], near.at[place], peer)
    sender.finish([copy for copy, _ in waves])
    own.wait()
    for store in stores:
        store.wait()


def final_exchange(rows, pairs):
    halves = [half for half, _ in pairs]
    dims = [dim for _, dim in pairs]
    n = len(pairs)
    outs = [jax.ShapeDtypeStruct((6 * rows.shape[0], rows.shape[1]), rows.dtype)]
    outs += [full_shape(half, dim) for half, dim in pairs]
    copies = 16 + 1 + n
    return pl.pallas_call(
        functools.partial(final_kernel_exchange, n, dims),
        out_shape=outs,
        in_specs=[VM] + [ANY] * n,
        out_specs=[ANY] * (n + 1),
        scratch_shapes=[pltpu.VMEM(half.shape, half.dtype) for half in halves]
        + [pltpu.SemaphoreType.DMA((copies,))] * 2
        + [pltpu.SemaphoreType.DMA((n + 1,))] * 2,
        compiler_params=pltpu.CompilerParams(collective_id=2, has_side_effects=True, vmem_limit_bytes=32 << 20),
        name="final_exchange",
    )(rows, *halves)


E_ENC = 32
E_DEC = 4


def enc_kernel(idx, q, wk, wv, go, near, bias, out, table, g, qk, mg):
    i = pl.program_id(0)
    steps = pl.num_programs(0)
    nodes = q.shape[0]
    heads2 = q.shape[1] // 128
    lane = lax.broadcasted_iota(jnp.int32, (1, 128), 1)
    low = lane < 64

    @pl.when(i == 0)
    def _():
        band = go.shape[0]
        for part, ref in enumerate((near.at[0:band], go, near.at[band:])):
            @pl.loop(0, band // 128)
            def _(b):
                r = pl.multiple_of(b * 128, 128)
                table[pl.ds(part * band + r, 128), 0, :] = ref[pl.ds(r, 128), :].astype(jnp.float32)
        for c in range(heads2):
            qc = q[:, c * 128:(c + 1) * 128].astype(jnp.float32)
            wc = wk[:, c * 128:(c + 1) * 128]
            for par in range(2):
                qm = jnp.where(low if par == 0 else ~low, qc, 0.0).astype(jnp.bfloat16)
                r = lax.dot_general(qm, wc, (((1,), (1,)), ((), ())), preferred_element_type=jnp.float32)
                qk[2 * c + par] = (r * SCALE).astype(jnp.bfloat16)

    rows = NB * E_ENC
    for r in range(rows):
        g[r:r + 1, :] = table[idx[i * rows + r]]
    gb = g[...].astype(jnp.bfloat16)
    n0 = pl.multiple_of(i * NB, NB)
    qb = qk[:, pl.ds(n0, NB), :].reshape(heads2 * 2 * NB, 128)
    s = lax.dot_general(qb, gb, (((1,), (1,)), ((), ())), preferred_element_type=jnp.float32)
    rn = lax.broadcasted_iota(jnp.int32, s.shape, 0) % NB
    cn = lax.broadcasted_iota(jnp.int32, s.shape, 1) // E_ENC
    s = jnp.where(rn == cn, s + bias[0], NEGATIVE)
    p = jnp.exp(s)
    l = jnp.sum(p, axis=-1, keepdims=True)
    m = jnp.dot(p.astype(jnp.bfloat16), gb, preferred_element_type=jnp.float32) / l
    mg[:, pl.ds(n0, NB), :] = m.astype(jnp.bfloat16).reshape(heads2 * 2, NB, 128)

    @pl.when(i == steps - 1)
    def _():
        for c in range(heads2):
            wc = wv[:, c * 128:(c + 1) * 128]
            a = jnp.dot(mg[2 * c], wc, preferred_element_type=jnp.float32)
            b = jnp.dot(mg[2 * c + 1], wc, preferred_element_type=jnp.float32)
            out[:, c * 128:(c + 1) * 128] = jnp.where(low, a, b).astype(jnp.bfloat16)

def enc_attention(q, wk, wv, go, near, sources, counts):
    nodes, width = q.shape
    slots = sources.shape[1]
    steps = nodes // NB
    live = jnp.arange(slots, dtype=jnp.int32)[None, :] < counts[:, None]
    bias = jnp.where(live, 0.0, NEGATIVE).astype(jnp.float32).reshape(steps, 1, NB * slots)
    full = lambda a: pl.BlockSpec(a.shape, lambda i, s: (0,) * a.ndim, pipeline_mode=pl.Buffered(1))
    return pl.pallas_call(
        enc_kernel,
        out_shape=jax.ShapeDtypeStruct((nodes, width), jnp.bfloat16),
        grid_spec=pltpu.PrefetchScalarGridSpec(
            num_scalar_prefetch=1, grid=(steps,),
            in_specs=[full(q), full(wk), full(wv), full(go), full(near),
                      pl.BlockSpec((1, 1, NB * slots), lambda i, s: (i, 0, 0))],
            out_specs=pl.BlockSpec((nodes, width), lambda i, s: (0, 0)),
            scratch_shapes=[
                pltpu.VMEM((3 * go.shape[0], 1, 128), jnp.float32),
                pltpu.VMEM((NB * slots, 128), jnp.float32),
                pltpu.VMEM((width // 64, nodes, 128), jnp.bfloat16),
                pltpu.VMEM((width // 64, nodes, 128), jnp.bfloat16)]),
        compiler_params=pltpu.CompilerParams(dimension_semantics=("arbitrary",), vmem_limit_bytes=48 << 20),
        cost_estimate=pl.CostEstimate(flops=4 << 30, bytes_accessed=8 << 20, transcendentals=4 << 20),
        name="enc_attention",
    )(sources.reshape(-1), q, wk, wv, go, near, bias)


def win_kernel(q, k, v, ones, out, p):
    nodes = q.shape[0]
    span = p.shape[-1]
    lane = lax.broadcasted_iota(jnp.int32, (1, 128), 1)
    low = lane < 64
    for b in range(nodes // QB):
        s0 = b * QB
        kb = k[s0:s0 + span, :]
        ve = jnp.concatenate((v[s0:s0 + span, :], ones[s0:s0 + span, :]), axis=1)
        qc = q[s0:s0 + QB, :].astype(jnp.float32) * SCALE
        res = []
        for par in range(2):
            qm = jnp.where(low if par == 0 else ~low, qc, 0.0).astype(jnp.bfloat16)
            for t in range(0, span, 256):
                w = min(256, span - t)
                s = lax.dot_general(qm, kb[t:t + w, :], (((1,), (1,)), ((), ())), preferred_element_type=jnp.float32)
                e = jnp.exp(s)
                if t < QB or t + w - 1 > 2 * HALF_WIN:
                    d = lax.broadcasted_iota(jnp.int32, s.shape, 1) + t - lax.broadcasted_iota(jnp.int32, s.shape, 0)
                    e = jnp.where((d >= 0) & (d <= 2 * HALF_WIN), e, 0.0)
                p[2*b+par, :, t:t + w] = e.astype(jnp.bfloat16)
            o = jnp.dot(p[2*b+par], ve, preferred_element_type=jnp.float32)
            res.append(o[:, :128] / o[:, 128:])
        out[s0:s0 + QB, :] = jnp.where(low, res[0], res[1]).astype(jnp.bfloat16)

def window(q, k, v, ones):
    nodes, width = q.shape
    span = -(-(QB + 2 * HALF_WIN) // 128) * 128
    keys = k.shape[0]
    return pl.pallas_call(
        win_kernel, out_shape=jax.ShapeDtypeStruct((nodes, width), jnp.bfloat16),
        grid=(width // 128,),
        in_specs=[pl.BlockSpec((nodes, 128), lambda c: (0, c)), pl.BlockSpec((keys, 128), lambda c: (0, c)),
                  pl.BlockSpec((keys, 128), lambda c: (0, c)), pl.BlockSpec((keys, 128), lambda c: (0, 0))],
        out_specs=pl.BlockSpec((nodes, 128), lambda c: (0, c)),
        scratch_shapes=[pltpu.VMEM((2*nodes//QB, QB, span), jnp.bfloat16)],
        compiler_params=pltpu.CompilerParams(dimension_semantics=("arbitrary",), vmem_limit_bytes=48 << 20),
        name="window_attention")(q, k, v, ones)


def dec_kernel(idx, cnt, x, wk, wv, gs, wq, wo, out, table, q3, prod, sc, mix3, seg):
    i = pl.program_id(0)
    tsteps = table.shape[0] // RB
    lane = lax.broadcasted_iota(jnp.int32, (1, 128), 1)

    @pl.when(i == 0)
    def _():
        r = lax.broadcasted_iota(jnp.int32, (128, 128), 0) // 64
        c = lax.broadcasted_iota(jnp.int32, (128, 128), 1) // 64
        seg[...] = jnp.where(r == c, 1.0, 0.0).astype(jnp.bfloat16)

    @pl.when(i < tsteps)
    def _():
        xf = x[...].astype(jnp.float32)
        cen = xf - jnp.mean(xf, axis=-1, keepdims=True)
        var = jnp.mean(cen * cen, axis=-1, keepdims=True)
        xn = (cen * lax.rsqrt(var + EPSILON)).astype(jnp.bfloat16)
        r0 = pl.multiple_of(i * RB, RB)
        for part, w in enumerate((wk, wk, wv, wv)):
            kv = jnp.dot(xn, w[:, (part % 2) * 512:(part % 2 + 1) * 512], preferred_element_type=jnp.float32)
            for s in range(4):
                table[pl.ds(r0, RB), part * 4 + s, :] = kv[:, s * 128:(s + 1) * 128]

    @pl.when(i >= tsteps)
    def _():
        b = i - tsteps
        g0 = b * GB
        gb = gs[...]
        qf = jnp.dot(gb, wq[...], preferred_element_type=jnp.float32) * SCALE
        for s in range(8):
            q3[:, s, :] = qf[:, s * 128:(s + 1) * 128]
        for g in range(GB):
            qv = q3[g]
            for e in range(E_DEC):
                prod[e, g] = qv * table[idx[(g0 + g) * E_DEC + e], 0:8, :]
        pm = prod[...].reshape(E_DEC * GB * 8, 128).astype(jnp.bfloat16)
        sc[...] = jnp.exp(jnp.dot(pm, seg[...], preferred_element_type=jnp.float32)).reshape(E_DEC, GB, 8, 128)
        for g in range(GB):
            c = cnt[g0 + g]
            tot = None
            acc = None
            for e in range(E_DEC):
                pe = sc[e, g]
                if e > 0:
                    pe = jnp.where(e < c, pe, 0.0)
                pv = pe * table[idx[(g0 + g) * E_DEC + e], 8:16, :]
                tot = pe if e == 0 else tot + pe
                acc = pv if e == 0 else acc + pv
            mix3[g] = acc / tot
        o = gb.astype(jnp.float32)
        m2 = jnp.concatenate([mix3[:, s, :] for s in range(8)], axis=1).astype(jnp.bfloat16)
        o = o + jnp.dot(m2, wo[...], preferred_element_type=jnp.float32)
        out[...] = o[:, :out.shape[1]].astype(jnp.bfloat16)

def decode(x, wk, wv, gs, wq, wo, sources, counts, variables):
    rows, width = x.shape
    grid_rows = gs.shape[0]
    tsteps = rows // RB
    steps = tsteps + grid_rows // GB
    full = lambda a: pl.BlockSpec(a.shape, lambda i, *_: (0,) * a.ndim, pipeline_mode=pl.Buffered(1))
    late = lambda i, *_: (jnp.maximum(i - tsteps, 0), 0)
    return pl.pallas_call(
        dec_kernel,
        out_shape=jax.ShapeDtypeStruct((grid_rows, variables), jnp.bfloat16),
        grid_spec=pltpu.PrefetchScalarGridSpec(
            num_scalar_prefetch=2, grid=(steps,),
            in_specs=[pl.BlockSpec((RB, width), lambda i, *_: (jnp.minimum(i, tsteps - 1), 0)),
                      full(wk), full(wv),
                      pl.BlockSpec((GB, 128), late), full(wq), full(wo)],
            out_specs=pl.BlockSpec((GB, variables), late),
            scratch_shapes=[
                pltpu.VMEM((rows, 16, 128), jnp.float32),
                pltpu.VMEM((GB, 8, 128), jnp.float32),
                pltpu.VMEM((E_DEC, GB, 8, 128), jnp.float32),
                pltpu.VMEM((E_DEC, GB, 8, 128), jnp.float32),
                pltpu.VMEM((GB, 8, 128), jnp.float32),
                pltpu.VMEM((128, 128), jnp.bfloat16)]),
        compiler_params=pltpu.CompilerParams(dimension_semantics=("arbitrary",), vmem_limit_bytes=56 << 20),
        name="dec_attention",
    )(sources.reshape(-1), counts, x, wk, wv, gs, wq, wo)


def local(
    grid_state,
    hidden_state,
    encoder_sources,
    encoder_counts,
    decoder_sources,
    decoder_counts,
    encoder_keys,
    encoder_values,
    encoder_query,
    encoder_output,
    window_query,
    window_keys,
    window_values,
    window_output,
    feed_up,
    feed_down,
    decoder_query,
    decoder_keys,
    decoder_values,
    decoder_output,
):
    band, head, _, _ = places()
    bands = lax.axis_size("band")
    band_nodes, half_width = hidden_state.shape
    nodes = band_nodes // 2
    grid_count, variables = grid_state.shape
    half_grid = grid_count // 2
    short = 128 - variables
    widen = lambda w: jnp.pad(w, ((0, short), (0, 0)))
    grid = jnp.pad(grid_state, ((0, 0), (0, short)))
    near_grid, state, enc_k, enc_v, enc_q, enc_o, win_q, win_k, win_v, win_o, dec_q, dec_o = start_exchange(
        grid, hidden_state,
        [(widen(encoder_keys), 1), (widen(encoder_values), 1), (encoder_query, 1), (encoder_output, 0),
         (window_query, 1), (window_keys, 1), (window_values, 1), (window_output, 0),
         (widen(decoder_query), 1), (jnp.pad(decoder_output, ((0, 0), (0, short))), 0)],
    )
    my_rows = lambda a, size: lax.dynamic_slice_in_dim(a, head * size, size, 0)
    query = project(layer_norm(state), enc_q)
    mix = enc_attention(query, enc_k, enc_v, grid, near_grid, my_rows(encoder_sources, nodes), my_rows(encoder_counts, nodes))
    mid = (state.astype(jnp.float32) + jnp.dot(mix, enc_o, preferred_element_type=jnp.float32)).astype(jnp.bfloat16)
    normed = layer_norm(mid)
    span = nodes + 2 * HALF_WIN
    span_rows = nodes - QB + -(-(QB + 2 * HALF_WIN) // 128) * 128
    near, up, down = window_exchange(normed, span_rows, [(feed_up, 1), (feed_down, 0)])
    place = jnp.arange(span_rows, dtype=jnp.int32)
    node = band * band_nodes + head * nodes - HALF_WIN + place
    live = ((place < span) & (node >= 0) & (node < bands * band_nodes))[:, None]
    near = jnp.where(live, near, jnp.zeros_like(near))
    ones = jnp.broadcast_to(live, (span_rows, 128)).astype(jnp.bfloat16)
    mixed = window(project(normed, win_q), project(near, win_k), project(near, win_v), ones)
    att = (mid.astype(jnp.float32) + jnp.dot(mixed, win_o, preferred_element_type=jnp.float32)).astype(jnp.bfloat16)
    inner = jax.nn.gelu(
        jnp.dot(layer_norm(att), up, preferred_element_type=jnp.float32), approximate=True
    ).astype(jnp.bfloat16)
    final = (att.astype(jnp.float32) + jnp.dot(inner, down, preferred_element_type=jnp.float32)).astype(jnp.bfloat16)
    near_final, dec_k, dec_v = final_exchange(final, [(decoder_keys, 1), (decoder_values, 1)])
    hidden_final = lax.dynamic_slice(near_final, (band_nodes, head * half_width), (band_nodes, half_width))
    sources = my_rows(decoder_sources, half_grid) - (band - 1) * band_nodes
    grid_next = decode(near_final, dec_k, dec_v, my_rows(grid, half_grid), dec_q, dec_o, sources,
                       my_rows(decoder_counts, half_grid), variables)
    return (grid_next, hidden_final)


def solution(mesh):
    in_specs = (
        P("band", None),
        P("band", "head"),
        P("band", None),
        P("band"),
        P("band", None),
        P("band"),
        P(None, "head"),
        P(None, "head"),
        P(None, "head"),
        P("head", None),
        P(None, "head"),
        P(None, "head"),
        P(None, "head"),
        P("head", None),
        P(None, "head"),
        P("head", None),
        P(None, "head"),
        P(None, "head"),
        P(None, "head"),
        P("head", None),
    )
    out_specs = (P(("band", "head"), None), P("band", "head"))
    return jax.shard_map(local, mesh=mesh, in_specs=in_specs, out_specs=out_specs, check_vma=False)
```

```python
import functools

import jax
import jax.numpy as jnp
from jax import lax
from jax.experimental import pallas as pl
from jax.experimental.pallas import tpu as pltpu
from jax.sharding import PartitionSpec as P

HALF_WIN = 560
HEAD_DIM = 64
EPSILON = 1e-05
NEGATIVE = -1e30
SCALE = HEAD_DIM**-0.5
LOG2E = 1.4426950408889634
MESH = pl.DeviceIdType.MESH
NB = 16
QB = 128
GB = 128
UN = 16
RB = 256
ANY = pl.BlockSpec(memory_space=pltpu.HBM)
VM = pl.BlockSpec(memory_space=pltpu.VMEM)


def layer_norm(matrix):
    as_float = matrix.astype(jnp.float32)
    centred = as_float - jnp.mean(as_float, axis=-1, keepdims=True)
    variance = jnp.mean(centred * centred, axis=-1, keepdims=True)
    return (centred * lax.rsqrt(variance + EPSILON)).astype(jnp.bfloat16)


def project(matrix, weight):
    return jnp.dot(matrix, weight, preferred_element_type=jnp.float32).astype(jnp.bfloat16)


def places():
    band = lax.axis_index("band")
    head = lax.axis_index("head")
    count = lax.axis_size("band")
    left = lax.rem(band + count - 1, count)
    right = lax.rem(band + 1, count)
    return band, head, left, right


def greet(others):
    barrier = pltpu.get_barrier_semaphore()
    for other in others:
        pl.semaphore_signal(barrier, inc=1, device_id=other, device_id_type=MESH)
    pl.semaphore_wait(barrier, len(others))


class Sender:
    def __init__(self, send_sem, recv_sem):
        self.send_sem, self.recv_sem, self.used, self.open = send_sem, recv_sem, 0, []

    def send(self, src, dst, device):
        n = self.used
        self.used += 1
        copy = pltpu.make_async_remote_copy(
            src_ref=src, dst_ref=dst, send_sem=self.send_sem.at[n], recv_sem=self.recv_sem.at[n],
            device_id=device, device_id_type=MESH)
        copy.start()
        self.open.append(copy)
        return copy

    def finish(self, received=()):
        for copy in self.open:
            copy.wait_send()
            if not any(copy is other for other in received):
                copy.wait_recv()


def half_of(ref, dim, index):
    size = ref.shape[dim] // 2
    part = pl.ds(pl.multiple_of(index * size, size), size)
    return ref.at[part] if dim == 0 else ref.at[:, part]


def relay(near, source, width, sides, sender, me, band, left, right, head, chunks):
    step = width // 2 // chunks
    waves = []
    for c in range(chunks):
        own = pl.ds(pl.multiple_of(head * (width // 2) + c * step, step), step)
        for side, other in ((sides[0], right), (sides[1], left)):
            rows = pl.ds(pl.multiple_of(side * width + head * (width // 2) + c * step, step), step)
            waves.append((sender.send(source(own, c, step), near.at[rows], (other, head)), rows))
    return waves


def start_kernel(n_pair, dims, *refs):
    grid, state = refs[0], refs[1]
    halves = refs[2 : 2 + n_pair]
    near, whole = refs[2 + n_pair], refs[3 + n_pair]
    fulls = refs[4 + n_pair : 4 + 2 * n_pair]
    rest = refs[4 + 2 * n_pair :]
    state_hold = rest[0]
    holds = rest[1 : 1 + n_pair]
    send_sem, recv_sem, load_sem, store_sem = rest[1 + n_pair :]
    band, head, left, right = places()
    peer = (band, 1 - head)
    loads = [pltpu.make_async_copy(half_of(state, 0, head), state_hold, load_sem.at[n_pair])]
    loads += [pltpu.make_async_copy(h, v, load_sem.at[n]) for n, (h, v) in enumerate(zip(halves, holds))]
    for load in loads:
        load.start()
    greet([peer, (left, head), (right, head)])
    sender = Sender(send_sem, recv_sem)
    waves = relay(near, lambda own, c, step: grid.at[own], grid.shape[0], (0, 1), sender, None, band, left, right, head, 4)
    sender.send(half_of(state, 0, 1 - head), half_of(whole, 1, head), peer)
    for n in range(n_pair):
        sender.send(halves[n], half_of(fulls[n], dims[n], head), peer)
    stores = [pltpu.make_async_copy(state_hold, half_of(whole, 1, head), store_sem.at[n_pair])]
    stores += [pltpu.make_async_copy(holds[n], half_of(fulls[n], dims[n], head), store_sem.at[n]) for n in range(n_pair)]
    for load, store in zip(loads, stores):
        load.wait()
        store.start()
    for copy, rows in waves:
        copy.wait_recv()
        sender.send(near.at[rows], near.at[rows], peer)
    sender.finish([copy for copy, _ in waves])
    for store in stores:
        store.wait()


def full_shape(half, dim):
    shape = list(half.shape)
    shape[dim] *= 2
    return jax.ShapeDtypeStruct(tuple(shape), half.dtype)


def start_exchange(grid, state, pairs):
    halves = [half for half, _ in pairs]
    dims = [dim for _, dim in pairs]
    n = len(pairs)
    nodes, width = state.shape
    outs = [jax.ShapeDtypeStruct((2 * grid.shape[0], grid.shape[1]), grid.dtype),
            jax.ShapeDtypeStruct((nodes // 2, width * 2), state.dtype)]
    outs += [full_shape(half, dim) for half, dim in pairs]
    copies = 16 + 1 + n
    return pl.pallas_call(
        functools.partial(start_kernel, n, dims),
        out_shape=outs,
        in_specs=[VM] + [ANY] * (n + 1),
        out_specs=[ANY] * (n + 2),
        scratch_shapes=[pltpu.VMEM((nodes // 2, width), state.dtype)]
        + [pltpu.VMEM(half.shape, half.dtype) for half in halves]
        + [pltpu.SemaphoreType.DMA((copies,))] * 2
        + [pltpu.SemaphoreType.DMA((n + 1,))] * 2,
        compiler_params=pltpu.CompilerParams(collective_id=0, has_side_effects=True, vmem_limit_bytes=60 << 20),
        name="start_exchange",
    )(grid, state, *halves)


def window_kernel_exchange(n_pair, dims, *refs):
    rows = refs[0]
    halves = refs[1 : 1 + n_pair]
    span = refs[1 + n_pair]
    fulls = refs[2 + n_pair : 2 + 2 * n_pair]
    rest = refs[2 + 2 * n_pair :]
    holds = rest[:n_pair]
    send_sem, recv_sem, load_sem, store_sem = rest[n_pair:]
    band, head, left, right = places()
    count = rows.shape[0]
    extra = HALF_WIN - count
    after = HALF_WIN + count
    peer = (band, 1 - head)
    across = (lax.rem(band + lax.axis_size("band") + 2 * head - 1, lax.axis_size("band")), 1 - head)
    loads = [pltpu.make_async_copy(h, v, load_sem.at[n]) for n, (h, v) in enumerate(zip(halves, holds))]
    for load in loads:
        load.start()
    own = pltpu.make_async_copy(rows, span.at[pl.ds(HALF_WIN, count)], store_sem.at[n_pair])
    own.start()
    greet([peer, (left, head), (right, head), across])
    sender = Sender(send_sem, recv_sem)
    sender.send(rows, span.at[pl.ds(pl.multiple_of(after + head * (extra - after), 16), count)], across)
    sender.send(rows.at[pl.ds(count - extra, extra)], span.at[pl.ds(0, extra)], (right, head))
    sender.send(rows.at[pl.ds(0, extra)], span.at[pl.ds(after + count, extra)], (left, head))
    sender.send(rows, span.at[pl.ds(pl.multiple_of(extra + head * (after - extra), 16), count)], peer)
    for n in range(n_pair):
        sender.send(halves[n], half_of(fulls[n], dims[n], head), peer)
    stores = [pltpu.make_async_copy(holds[n], half_of(fulls[n], dims[n], head), store_sem.at[n]) for n in range(n_pair)]
    for load, store in zip(loads, stores):
        load.wait()
        store.start()
    sender.finish()
    own.wait()
    for store in stores:
        store.wait()


def window_exchange(rows, span_rows, pairs):
    halves = [half for half, _ in pairs]
    dims = [dim for _, dim in pairs]
    n = len(pairs)
    outs = [jax.ShapeDtypeStruct((span_rows, rows.shape[1]), rows.dtype)]
    outs += [full_shape(half, dim) for half, dim in pairs]
    copies = 4 + n
    return pl.pallas_call(
        functools.partial(window_kernel_exchange, n, dims),
        out_shape=outs,
        in_specs=[VM] + [ANY] * n,
        out_specs=[ANY] * (n + 1),
        scratch_shapes=[pltpu.VMEM(half.shape, half.dtype) for half in halves]
        + [pltpu.SemaphoreType.DMA((copies,))] * 2
        + [pltpu.SemaphoreType.DMA((n + 1,))] * 2,
        compiler_params=pltpu.CompilerParams(collective_id=1, has_side_effects=True, vmem_limit_bytes=60 << 20),
        name="window_exchange",
    )(rows, *halves)


def final_kernel_exchange(n_pair, dims, *refs):
    rows = refs[0]
    halves = refs[1 : 1 + n_pair]
    near = refs[1 + n_pair]
    fulls = refs[2 + n_pair : 2 + 2 * n_pair]
    rest = refs[2 + 2 * n_pair :]
    holds = rest[:n_pair]
    send_sem, recv_sem, load_sem, store_sem = rest[n_pair:]
    band, head, left, right = places()
    count = rows.shape[0]
    peer = (band, 1 - head)
    loads = [pltpu.make_async_copy(h, v, load_sem.at[n]) for n, (h, v) in enumerate(zip(halves, holds))]
    for load in loads:
        load.start()
    mine = pl.ds(pl.multiple_of(2 * count + head * count, count), count)
    own = pltpu.make_async_copy(rows, near.at[mine], store_sem.at[n_pair])
    own.start()
    greet([peer, (left, head), (right, head)])
    sender = Sender(send_sem, recv_sem)
    waves = relay(near, lambda o, c, step: rows.at[pl.ds(c * step, step)], 2 * count, (0, 2), sender, None, band, left, right, head, 4)
    sender.send(rows, near.at[mine], peer)
    for n in range(n_pair):
        sender.send(halves[n], half_of(fulls[n], dims[n], head), peer)
    stores = [pltpu.make_async_copy(holds[n], half_of(fulls[n], dims[n], head), store_sem.at[n]) for n in range(n_pair)]
    for load, store in zip(loads, stores):
        load.wait()
        store.start()
    for copy, place in waves:
        copy.wait_recv()
        sender.send(near.at[place], near.at[place], peer)
    sender.finish([copy for copy, _ in waves])
    own.wait()
    for store in stores:
        store.wait()


def final_exchange(rows, pairs):
    halves = [half for half, _ in pairs]
    dims = [dim for _, dim in pairs]
    n = len(pairs)
    outs = [jax.ShapeDtypeStruct((6 * rows.shape[0], rows.shape[1]), rows.dtype)]
    outs += [full_shape(half, dim) for half, dim in pairs]
    copies = 16 + 1 + n
    return pl.pallas_call(
        functools.partial(final_kernel_exchange, n, dims),
        out_shape=outs,
        in_specs=[VM] + [ANY] * n,
        out_specs=[ANY] * (n + 1),
        scratch_shapes=[pltpu.VMEM(half.shape, half.dtype) for half in halves]
        + [pltpu.SemaphoreType.DMA((copies,))] * 2
        + [pltpu.SemaphoreType.DMA((n + 1,))] * 2,
        compiler_params=pltpu.CompilerParams(collective_id=2, has_side_effects=True, vmem_limit_bytes=60 << 20),
        name="final_exchange",
    )(rows, *halves)


E_ENC = 32
E_DEC = 4


def enc_kernel(idx, q, wk, wv, go, near, bias, out, table, g, qk, mg):
    i = pl.program_id(0)
    steps = pl.num_programs(0)
    nodes = q.shape[0]
    heads2 = q.shape[1] // 128
    lane = lax.broadcasted_iota(jnp.int32, (1, 128), 1)
    low = lane < 64

    @pl.when(i == 0)
    def _():
        band = go.shape[0]
        for part, ref in enumerate((near.at[0:band], go, near.at[band:])):
            @pl.loop(0, band // 128)
            def _(b):
                r = pl.multiple_of(b * 128, 128)
                table[pl.ds(part * band + r, 128), 0, :] = ref[pl.ds(r, 128), :].astype(jnp.float32)
        for c in range(heads2):
            qc = q[:, c * 128:(c + 1) * 128].astype(jnp.float32)
            wc = wk[:, c * 128:(c + 1) * 128]
            for par in range(2):
                qm = jnp.where(low if par == 0 else ~low, qc, 0.0).astype(jnp.bfloat16)
                r = lax.dot_general(qm, wc, (((1,), (1,)), ((), ())), preferred_element_type=jnp.float32)
                qk[2 * c + par] = (r * SCALE).astype(jnp.bfloat16)

    rows = NB * E_ENC
    for r in range(rows):
        g[r:r + 1, :] = table[idx[i * rows + r]]
    gb = g[...].astype(jnp.bfloat16)
    n0 = pl.multiple_of(i * NB, NB)
    qb = qk[:, pl.ds(n0, NB), :].reshape(heads2 * 2 * NB, 128)
    s = lax.dot_general(qb, gb, (((1,), (1,)), ((), ())), preferred_element_type=jnp.float32)
    rn = lax.broadcasted_iota(jnp.int32, s.shape, 0) % NB
    cn = lax.broadcasted_iota(jnp.int32, s.shape, 1) // E_ENC
    s = jnp.where(rn == cn, s + bias[0], NEGATIVE)
    p = jnp.exp(s)
    l = jnp.sum(p, axis=-1, keepdims=True)
    m = jnp.dot(p.astype(jnp.bfloat16), gb, preferred_element_type=jnp.float32) / l
    mg[:, pl.ds(n0, NB), :] = m.astype(jnp.bfloat16).reshape(heads2 * 2, NB, 128)

    @pl.when(i == steps - 1)
    def _():
        for c in range(heads2):
            wc = wv[:, c * 128:(c + 1) * 128]
            a = jnp.dot(mg[2 * c], wc, preferred_element_type=jnp.float32)
            b = jnp.dot(mg[2 * c + 1], wc, preferred_element_type=jnp.float32)
            out[:, c * 128:(c + 1) * 128] = jnp.where(low, a, b).astype(jnp.bfloat16)

def enc_attention(q, wk, wv, go, near, sources, counts):
    nodes, width = q.shape
    slots = sources.shape[1]
    steps = nodes // NB
    live = jnp.arange(slots, dtype=jnp.int32)[None, :] < counts[:, None]
    bias = jnp.where(live, 0.0, NEGATIVE).astype(jnp.float32).reshape(steps, 1, NB * slots)
    full = lambda a: pl.BlockSpec(a.shape, lambda i, s: (0,) * a.ndim, pipeline_mode=pl.Buffered(1))
    return pl.pallas_call(
        enc_kernel,
        out_shape=jax.ShapeDtypeStruct((nodes, width), jnp.bfloat16),
        grid_spec=pltpu.PrefetchScalarGridSpec(
            num_scalar_prefetch=1, grid=(steps,),
            in_specs=[full(q), full(wk), full(wv), full(go), full(near),
                      pl.BlockSpec((1, 1, NB * slots), lambda i, s: (i, 0, 0))],
            out_specs=pl.BlockSpec((nodes, width), lambda i, s: (0, 0)),
            scratch_shapes=[
                pltpu.VMEM((3 * go.shape[0], 1, 128), jnp.float32),
                pltpu.VMEM((NB * slots, 128), jnp.float32),
                pltpu.VMEM((width // 64, nodes, 128), jnp.bfloat16),
                pltpu.VMEM((width // 64, nodes, 128), jnp.bfloat16)]),
        compiler_params=pltpu.CompilerParams(dimension_semantics=("arbitrary",), vmem_limit_bytes=48 << 20),
        cost_estimate=pl.CostEstimate(flops=4 << 30, bytes_accessed=8 << 20, transcendentals=4 << 20),
        name="enc_attention",
    )(sources.reshape(-1), q, wk, wv, go, near, bias)


def win_kernel(q, k, v, ones, out, p):
    nodes = q.shape[0]
    span = p.shape[-1]
    lane = lax.broadcasted_iota(jnp.int32, (1, 128), 1)
    low = lane < 64
    for b in range(nodes // QB):
        s0 = b * QB
        kb = k[s0:s0 + span, :]
        ve = jnp.concatenate((v[s0:s0 + span, :], ones[s0:s0 + span, :]), axis=1)
        qc = q[s0:s0 + QB, :].astype(jnp.float32) * SCALE
        res = []
        for par in range(2):
            qm = jnp.where(low if par == 0 else ~low, qc, 0.0).astype(jnp.bfloat16)
            for t in range(0, span, 256):
                w = min(256, span - t)
                s = lax.dot_general(qm, kb[t:t + w, :], (((1,), (1,)), ((), ())), preferred_element_type=jnp.float32)
                e = jnp.exp(s)
                if t < QB or t + w - 1 > 2 * HALF_WIN:
                    d = lax.broadcasted_iota(jnp.int32, s.shape, 1) + t - lax.broadcasted_iota(jnp.int32, s.shape, 0)
                    e = jnp.where((d >= 0) & (d <= 2 * HALF_WIN), e, 0.0)
                p[2*b+par, :, t:t + w] = e.astype(jnp.bfloat16)
            o = jnp.dot(p[2*b+par], ve, preferred_element_type=jnp.float32)
            res.append(o[:, :128] / o[:, 128:])
        out[s0:s0 + QB, :] = jnp.where(low, res[0], res[1]).astype(jnp.bfloat16)

def window(q, k, v, ones):
    nodes, width = q.shape
    span = -(-(QB + 2 * HALF_WIN) // 128) * 128
    keys = k.shape[0]
    return pl.pallas_call(
        win_kernel, out_shape=jax.ShapeDtypeStruct((nodes, width), jnp.bfloat16),
        grid=(width // 128,),
        in_specs=[pl.BlockSpec((nodes, 128), lambda c: (0, c)), pl.BlockSpec((keys, 128), lambda c: (0, c)),
                  pl.BlockSpec((keys, 128), lambda c: (0, c)), pl.BlockSpec((keys, 128), lambda c: (0, 0))],
        out_specs=pl.BlockSpec((nodes, 128), lambda c: (0, c)),
        scratch_shapes=[pltpu.VMEM((2*nodes//QB, QB, span), jnp.bfloat16)],
        compiler_params=pltpu.CompilerParams(dimension_semantics=("arbitrary",), vmem_limit_bytes=48 << 20),
        name="window_attention")(q, k, v, ones)


def dec_kernel(idx, x, wk, wv, cnt, gs, wq, wo, out, table, q3, prod_a, held_a, prod_b, held_b, mix3, seg, live):
    i = pl.program_id(0)
    tsteps = table.shape[0] // (2 * RB)
    rows = table.shape[0] // 2
    lines = table.reshape(table.shape[0] * 8, 128)
    qlines = q3.reshape(GB * 8, 128)
    lives = live.reshape(E_DEC * GB, 128)
    mlines = mix3.reshape(GB * 8, 128)
    lane = lax.broadcasted_iota(jnp.int32, (1, 128), 1)

    @pl.when(i == 0)
    def _():
        r = lax.broadcasted_iota(jnp.int32, (128, 128), 0) // 64
        c = lax.broadcasted_iota(jnp.int32, (128, 128), 1) // 64
        seg[...] = jnp.where(r == c, 1.0, 0.0).astype(jnp.bfloat16)

    @pl.when(i < tsteps)
    def _():
        xf = x[...].astype(jnp.float32)
        cen = xf - jnp.mean(xf, axis=-1, keepdims=True)
        var = jnp.mean(cen * cen, axis=-1, keepdims=True)
        xn = (cen * lax.rsqrt(var + EPSILON)).astype(jnp.bfloat16)
        for part, w in enumerate((wk, wk, wv, wv)):
            kv = jnp.dot(xn, w[:, part % 2 * 512:part % 2 * 512 + 512], preferred_element_type=jnp.float32)
            for s in range(4):
                lines[pl.ds(i * (RB * 8) + (part // 2 * rows * 8 + part % 2 * 4 + s), RB, stride=8), :] = kv[:, s * 128:(s + 1) * 128]

    @pl.when(i >= tsteps)
    def _():
        b = i - tsteps
        g0 = b * GB
        gb = gs[...]
        qf = jnp.dot(gb, wq[...], preferred_element_type=jnp.float32) * (SCALE * LOG2E)
        for s in range(8):
            q3[:, s] = qf[:, s * 128:(s + 1) * 128].reshape(GB // 8, 8, 128)
        for e in range(E_DEC):
            live[e] = jnp.broadcast_to(jnp.where(cnt[...] > e, 1.0, 0.0), (GB, 128))

        def gather(o, prod, held):
            base = (g0 + o * UN) * E_DEC
            for j in range(UN):
                place = (j // 8) * 64 + j % 8
                qv = qlines[pl.ds(pl.multiple_of(o * (UN * 8), 64) + place, 8, stride=8), :]
                parts = []
                for e in range(E_DEC):
                    at = pl.multiple_of(idx[base + (j * E_DEC + e)], 8)
                    parts.append(qv * lines[pl.ds(at, 8), :])
                    held[j, e] = lines[pl.ds(at + rows * 8, 8), :]
                for h in range(E_DEC // 2):
                    prod[j, h] = jnp.concatenate(parts[2 * h:2 * h + 2], axis=0).astype(jnp.bfloat16)

        def mixing(o, prod, held):
            pm = prod[...].reshape(E_DEC * UN * 8, 128)
            sc = jnp.dot(pm, seg[...], preferred_element_type=jnp.float32).reshape(UN, E_DEC, 8, 128)
            for j in range(UN):
                tot = None
                for e in range(E_DEC):
                    pe = jnp.exp2(sc[j, e])
                    if e > 0:
                        pe = pe * lives[pl.ds(e * GB + (o * UN + j), 8, stride=0), :]
                    pv = pe * held[j, e]
                    tot = pe if e == 0 else tot + pe
                    acc = pv if e == 0 else acc + pv
                place = (j // 8) * 64 + j % 8
                mlines[pl.ds(pl.multiple_of(o * (UN * 8), 64) + place, 8, stride=8), :] = acc / tot

        rounds = GB // UN
        gather(0, prod_a, held_a)

        def both(o, carry):
            gather(2 * o + 1, prod_b, held_b)
            mixing(2 * o, prod_a, held_a)
            gather(2 * o + 2, prod_a, held_a)
            mixing(2 * o + 1, prod_b, held_b)
            return carry

        lax.fori_loop(0, rounds // 2 - 1, both, 0)
        gather(rounds - 1, prod_b, held_b)
        mixing(rounds - 2, prod_a, held_a)
        mixing(rounds - 1, prod_b, held_b)
        o = gb.astype(jnp.float32)
        m2 = jnp.concatenate([mix3[:, s].reshape(GB, 128) for s in range(8)], axis=1).astype(jnp.bfloat16)
        o = o + jnp.dot(m2, wo[...], preferred_element_type=jnp.float32)
        out[...] = o[:, :out.shape[1]].astype(jnp.bfloat16)

def decode(x, wk, wv, gs, wq, wo, sources, counts, variables):
    rows, width = x.shape
    grid_rows = gs.shape[0]
    tsteps = rows // RB
    steps = tsteps + grid_rows // GB
    full = lambda a: pl.BlockSpec(a.shape, lambda i, *_: (0,) * a.ndim, pipeline_mode=pl.Buffered(1))
    late = lambda i, *_: (jnp.maximum(i - tsteps, 0), 0)
    return pl.pallas_call(
        dec_kernel,
        out_shape=jax.ShapeDtypeStruct((grid_rows, variables), jnp.bfloat16),
        grid_spec=pltpu.PrefetchScalarGridSpec(
            num_scalar_prefetch=1, grid=(steps,),
            in_specs=[pl.BlockSpec((RB, width), lambda i, *_: (jnp.minimum(i, tsteps - 1), 0)),
                      full(wk), full(wv),
                      pl.BlockSpec((GB, 1), late), pl.BlockSpec((GB, 128), late), full(wq), full(wo)],
            out_specs=pl.BlockSpec((GB, variables), late),
            scratch_shapes=[
                pltpu.VMEM((2 * rows, 8, 128), jnp.float32),
                pltpu.VMEM((GB // 8, 8, 8, 128), jnp.float32),
                pltpu.VMEM((UN, E_DEC // 2, 16, 128), jnp.bfloat16),
                pltpu.VMEM((UN, E_DEC, 8, 128), jnp.float32),
                pltpu.VMEM((UN, E_DEC // 2, 16, 128), jnp.bfloat16),
                pltpu.VMEM((UN, E_DEC, 8, 128), jnp.float32),
                pltpu.VMEM((GB // 8, 8, 8, 128), jnp.float32),
                pltpu.VMEM((128, 128), jnp.bfloat16),
                pltpu.VMEM((E_DEC, GB, 128), jnp.float32)]),
        compiler_params=pltpu.CompilerParams(dimension_semantics=("arbitrary",), vmem_limit_bytes=56 << 20),
        name="dec_attention",
    )((sources * 8).reshape(-1), x, wk, wv, counts[:, None], gs, wq, wo)


def local(
    grid_state,
    hidden_state,
    encoder_sources,
    encoder_counts,
    decoder_sources,
    decoder_counts,
    encoder_keys,
    encoder_values,
    encoder_query,
    encoder_output,
    window_query,
    window_keys,
    window_values,
    window_output,
    feed_up,
    feed_down,
    decoder_query,
    decoder_keys,
    decoder_values,
    decoder_output,
):
    band, head, _, _ = places()
    bands = lax.axis_size("band")
    band_nodes, half_width = hidden_state.shape
    nodes = band_nodes // 2
    grid_count, variables = grid_state.shape
    half_grid = grid_count // 2
    short = 128 - variables
    widen = lambda w: jnp.pad(w, ((0, short), (0, 0)))
    grid = jnp.pad(grid_state, ((0, 0), (0, short)))
    near_grid, state, enc_k, enc_v, enc_q, enc_o, win_q, win_k, win_v, win_o, dec_q, dec_o = start_exchange(
        grid, hidden_state,
        [(widen(encoder_keys), 1), (widen(encoder_values), 1), (encoder_query, 1), (encoder_output, 0),
         (window_query, 1), (window_keys, 1), (window_values, 1), (window_output, 0),
         (widen(decoder_query), 1), (jnp.pad(decoder_output, ((0, 0), (0, short))), 0)],
    )
    my_rows = lambda a, size: lax.dynamic_slice_in_dim(a, head * size, size, 0)
    query = project(layer_norm(state), enc_q)
    mix = enc_attention(query, enc_k, enc_v, grid, near_grid, my_rows(encoder_sources, nodes), my_rows(encoder_counts, nodes))
    mid = (state.astype(jnp.float32) + jnp.dot(mix, enc_o, preferred_element_type=jnp.float32)).astype(jnp.bfloat16)
    normed = layer_norm(mid)
    span = nodes + 2 * HALF_WIN
    span_rows = nodes - QB + -(-(QB + 2 * HALF_WIN) // 128) * 128
    near, up, down = window_exchange(normed, span_rows, [(feed_up, 1), (feed_down, 0)])
    place = jnp.arange(span_rows, dtype=jnp.int32)
    node = band * band_nodes + head * nodes - HALF_WIN + place
    live = ((place < span) & (node >= 0) & (node < bands * band_nodes))[:, None]
    near = jnp.where(live, near, jnp.zeros_like(near))
    ones = jnp.broadcast_to(live, (span_rows, 128)).astype(jnp.bfloat16)
    mixed = window(project(normed, win_q), project(near, win_k), project(near, win_v), ones)
    att = (mid.astype(jnp.float32) + jnp.dot(mixed, win_o, preferred_element_type=jnp.float32)).astype(jnp.bfloat16)
    inner = jax.nn.gelu(
        jnp.dot(layer_norm(att), up, preferred_element_type=jnp.float32), approximate=True
    ).astype(jnp.bfloat16)
    final = (att.astype(jnp.float32) + jnp.dot(inner, down, preferred_element_type=jnp.float32)).astype(jnp.bfloat16)
    near_final, dec_k, dec_v = final_exchange(final, [(decoder_keys, 1), (decoder_values, 1)])
    hidden_final = lax.dynamic_slice(near_final, (band_nodes, head * half_width), (band_nodes, half_width))
    sources = my_rows(decoder_sources, half_grid) - (band - 1) * band_nodes
    grid_next = decode(near_final, dec_k, dec_v, my_rows(grid, half_grid), dec_q, dec_o, sources,
                       my_rows(decoder_counts, half_grid), variables)
    return (grid_next, hidden_final)


def solution(mesh):
    in_specs = (
        P("band", None),
        P("band", "head"),
        P("band", None),
        P("band"),
        P("band", None),
        P("band"),
        P(None, "head"),
        P(None, "head"),
        P(None, "head"),
        P("head", None),
        P(None, "head"),
        P(None, "head"),
        P(None, "head"),
        P("head", None),
        P(None, "head"),
        P("head", None),
        P(None, "head"),
        P(None, "head"),
        P(None, "head"),
        P("head", None),
    )
    out_specs = (P(("band", "head"), None), P("band", "head"))
    return jax.shard_map(local, mesh=mesh, in_specs=in_specs, out_specs=out_specs, check_vma=False)
```

```python
import functools

import jax
import jax.numpy as jnp
from jax import lax
from jax.experimental import pallas as pl
from jax.experimental.pallas import tpu as pltpu
from jax.sharding import PartitionSpec as P

HALF_WIN = 560
HEAD_DIM = 64
EPSILON = 1e-05
NEGATIVE = -1e30
SCALE = HEAD_DIM**-0.5
LOG2E = 1.4426950408889634
MESH = pl.DeviceIdType.MESH
NB = 16
QB = 128
GB = 128
UN = 16
ANY = pl.BlockSpec(memory_space=pltpu.HBM)
VM = pl.BlockSpec(memory_space=pltpu.VMEM)


def layer_norm(matrix):
    as_float = matrix.astype(jnp.float32)
    centred = as_float - jnp.mean(as_float, axis=-1, keepdims=True)
    variance = jnp.mean(centred * centred, axis=-1, keepdims=True)
    return (centred * lax.rsqrt(variance + EPSILON)).astype(jnp.bfloat16)


def project(matrix, weight):
    return jnp.dot(matrix, weight, preferred_element_type=jnp.float32).astype(jnp.bfloat16)


def places():
    band = lax.axis_index("band")
    head = lax.axis_index("head")
    count = lax.axis_size("band")
    left = lax.rem(band + count - 1, count)
    right = lax.rem(band + 1, count)
    return band, head, left, right


def greet(others):
    barrier = pltpu.get_barrier_semaphore()
    for other in others:
        pl.semaphore_signal(barrier, inc=1, device_id=other, device_id_type=MESH)
    pl.semaphore_wait(barrier, len(others))


class Sender:
    def __init__(self, send_sem, recv_sem):
        self.send_sem, self.recv_sem, self.used, self.open = send_sem, recv_sem, 0, []

    def send(self, src, dst, device):
        n = self.used
        self.used += 1
        copy = pltpu.make_async_remote_copy(
            src_ref=src, dst_ref=dst, send_sem=self.send_sem.at[n], recv_sem=self.recv_sem.at[n],
            device_id=device, device_id_type=MESH)
        copy.start()
        self.open.append(copy)
        return copy

    def finish(self, received=()):
        for copy in self.open:
            copy.wait_send()
            if not any(copy is other for other in received):
                copy.wait_recv()


def half_of(ref, dim, index):
    size = ref.shape[dim] // 2
    part = pl.ds(pl.multiple_of(index * size, size), size)
    return ref.at[part] if dim == 0 else ref.at[:, part]


def relay(near, source, width, sides, sender, me, band, left, right, head, chunks):
    step = width // 2 // chunks
    waves = []
    for c in range(chunks):
        own = pl.ds(pl.multiple_of(head * (width // 2) + c * step, step), step)
        for side, other in ((sides[0], right), (sides[1], left)):
            rows = pl.ds(pl.multiple_of(side * width + head * (width // 2) + c * step, step), step)
            waves.append((sender.send(source(own, c, step), near.at[rows], (other, head)), rows))
    return waves


def start_kernel(n_pair, dims, *refs):
    grid, state = refs[0], refs[1]
    halves = refs[2 : 2 + n_pair]
    near, whole = refs[2 + n_pair], refs[3 + n_pair]
    fulls = refs[4 + n_pair : 4 + 2 * n_pair]
    rest = refs[4 + 2 * n_pair :]
    state_hold = rest[0]
    holds = rest[1 : 1 + n_pair]
    send_sem, recv_sem, load_sem, store_sem = rest[1 + n_pair :]
    band, head, left, right = places()
    peer = (band, 1 - head)
    loads = [pltpu.make_async_copy(half_of(state, 0, head), state_hold, load_sem.at[n_pair])]
    loads += [pltpu.make_async_copy(h, v, load_sem.at[n]) for n, (h, v) in enumerate(zip(halves, holds))]
    for load in loads:
        load.start()
    greet([peer, (left, head), (right, head)])
    sender = Sender(send_sem, recv_sem)
    waves = relay(near, lambda own, c, step: grid.at[own], grid.shape[0], (0, 1), sender, None, band, left, right, head, 4)
    sender.send(half_of(state, 0, 1 - head), half_of(whole, 1, head), peer)
    for n in range(n_pair):
        sender.send(halves[n], half_of(fulls[n], dims[n], head), peer)
    stores = [pltpu.make_async_copy(state_hold, half_of(whole, 1, head), store_sem.at[n_pair])]
    stores += [pltpu.make_async_copy(holds[n], half_of(fulls[n], dims[n], head), store_sem.at[n]) for n in range(n_pair)]
    for load, store in zip(loads, stores):
        load.wait()
        store.start()
    for copy, rows in waves:
        copy.wait_recv()
        sender.send(near.at[rows], near.at[rows], peer)
    sender.finish([copy for copy, _ in waves])
    for store in stores:
        store.wait()


def full_shape(half, dim):
    shape = list(half.shape)
    shape[dim] *= 2
    return jax.ShapeDtypeStruct(tuple(shape), half.dtype)


def start_exchange(grid, state, pairs):
    halves = [half for half, _ in pairs]
    dims = [dim for _, dim in pairs]
    n = len(pairs)
    nodes, width = state.shape
    outs = [jax.ShapeDtypeStruct((2 * grid.shape[0], grid.shape[1]), grid.dtype),
            jax.ShapeDtypeStruct((nodes // 2, width * 2), state.dtype)]
    outs += [full_shape(half, dim) for half, dim in pairs]
    copies = 16 + 1 + n
    return pl.pallas_call(
        functools.partial(start_kernel, n, dims),
        out_shape=outs,
        in_specs=[VM] + [ANY] * (n + 1),
        out_specs=[ANY] * (n + 2),
        scratch_shapes=[pltpu.VMEM((nodes // 2, width), state.dtype)]
        + [pltpu.VMEM(half.shape, half.dtype) for half in halves]
        + [pltpu.SemaphoreType.DMA((copies,))] * 2
        + [pltpu.SemaphoreType.DMA((n + 1,))] * 2,
        compiler_params=pltpu.CompilerParams(collective_id=0, has_side_effects=True, vmem_limit_bytes=60 << 20),
        name="start_exchange",
    )(grid, state, *halves)


def span_kernel(n_pair, dims, *refs):
    rows, wq, wk, wv = refs[:4]
    halves = refs[4 : 4 + n_pair]
    q, k, v = refs[4 + n_pair : 7 + n_pair]
    fulls = refs[7 + n_pair : 7 + 2 * n_pair]
    span, hold_q, hold_k, hold_v = refs[7 + 2 * n_pair : 11 + 2 * n_pair]
    holds = refs[11 + 2 * n_pair : 11 + 3 * n_pair]
    send_sem, recv_sem, load_sem, store_sem = refs[11 + 3 * n_pair :]
    band, head, left, right = places()
    bands = lax.axis_size("band")
    count, width = rows.shape
    extra = HALF_WIN - count
    after = HALF_WIN + count
    chunks = 4
    step = count // chunks
    peer = (band, 1 - head)
    beside = (lax.rem(band + bands + 2 * head - 1, bands), 1 - head)
    weights = [pltpu.make_async_copy(w, hold, load_sem.at[n_pair + n]) for n, (w, hold) in enumerate(((wq, hold_q), (wk, hold_k), (wv, hold_v)))]
    for load in weights:
        load.start()
    loads = [pltpu.make_async_copy(h, hold, load_sem.at[n]) for n, (h, hold) in enumerate(zip(halves, holds))]
    for load in loads:
        load.start()
    greet([peer, (left, head), (right, head), beside])
    sender = Sender(send_sem, recv_sem)
    from_beside = extra + head * (after - extra)
    from_peer = after + head * (extra - after)
    first = sender.send(rows.at[pl.ds(count - extra, extra)], span.at[pl.ds(0, extra)], (right, head))
    last = sender.send(rows.at[pl.ds(0, extra)], span.at[pl.ds(after + count, extra)], (left, head))
    waves = [sender.send(rows.at[pl.ds(c * step, step)], span.at[pl.ds(pl.multiple_of(from_peer + c * step, 16), step)], beside)
             for c in range(chunks)]
    partner = sender.send(rows, span.at[pl.ds(pl.multiple_of(from_beside, 16), count)], peer)
    for n in range(n_pair):
        sender.send(halves[n], half_of(fulls[n], dims[n], head), peer)
    for load in weights:
        load.wait()

    def pair(x, place, size):
        node = band * (2 * count) + head * count - HALF_WIN + place + lax.broadcasted_iota(jnp.int32, (size, 1), 0)
        live = (node >= 0) & (node < bands * 2 * count)
        for w, o in ((hold_k, k), (hold_v, v)):
            o[pl.ds(place, size), :] = jnp.where(live, jnp.dot(x, w[...], preferred_element_type=jnp.float32), 0.0).astype(jnp.bfloat16)

    half = count // 2
    for b in range(2):
        x = rows[b * half:(b + 1) * half, :]
        q[b * half:(b + 1) * half, :] = jnp.dot(x, hold_q[...], preferred_element_type=jnp.float32).astype(jnp.bfloat16)
        pair(x, HALF_WIN + b * half, half)
    stores = [pltpu.make_async_copy(holds[n], half_of(fulls[n], dims[n], head), store_sem.at[n]) for n in range(n_pair)]
    for load, store in zip(loads, stores):
        load.wait()
        store.start()
    partner.wait_recv()
    for b in range(2):
        place = pl.multiple_of(from_peer + b * half, 16)
        pair(span[pl.ds(place, half), :], place, half)
    first.wait_recv()
    last.wait_recv()
    tail = span.shape[0] - after - count - extra
    pad = jnp.zeros((tail, width), rows.dtype)
    pair(span[0:extra, :], 0, extra)
    pair(jnp.concatenate((span[after + count:after + count + extra, :], pad), axis=0), after + count, extra + tail)
    for b in range(2):
        for c in range(b * chunks // 2, (b + 1) * chunks // 2):
            waves[c].wait_recv()
        place = pl.multiple_of(from_beside + b * half, 16)
        pair(span[pl.ds(place, half), :], place, half)
    sender.finish(waves + [first, last, partner])
    for store in stores:
        store.wait()


def window_span(rows, span_rows, wq, wk, wv, pairs):
    halves = [half for half, _ in pairs]
    dims = [dim for _, dim in pairs]
    n = len(pairs)
    outs = [jax.ShapeDtypeStruct((size, rows.shape[1]), rows.dtype) for size in (rows.shape[0], span_rows, span_rows)]
    outs += [full_shape(half, dim) for half, dim in pairs]
    copies = 7 + n
    return pl.pallas_call(
        functools.partial(span_kernel, n, dims),
        out_shape=outs,
        in_specs=[VM] + [ANY] * (n + 3),
        out_specs=[VM] * 3 + [ANY] * n,
        scratch_shapes=[pltpu.VMEM((span_rows, rows.shape[1]), rows.dtype)]
        + [pltpu.VMEM(w.shape, w.dtype) for w in (wq, wk, wv)]
        + [pltpu.VMEM(half.shape, half.dtype) for half in halves]
        + [pltpu.SemaphoreType.DMA((copies,))] * 2
        + [pltpu.SemaphoreType.DMA((n + 3,)), pltpu.SemaphoreType.DMA((n,))],
        compiler_params=pltpu.CompilerParams(collective_id=1, has_side_effects=True, vmem_limit_bytes=46 << 20),
        name="window_span",
    )(rows, wq, wk, wv, *halves)


def tables_kernel(rows, wk, wv, table, out, near, hold_k, hold_v, blocks, send_sem, recv_sem, load_sem, store_sem):
    band, head, left, right = places()
    count, width = rows.shape
    chunks = 4
    step = count // chunks
    peer = (band, 1 - head)
    lines = blocks.reshape(blocks.shape[0] * blocks.shape[1] * blocks.shape[2] * 8, 128)
    loads = [pltpu.make_async_copy(half, half_of(hold, 1, head), load_sem.at[n])
             for n, (half, hold) in enumerate(((wk, hold_k), (wv, hold_v)))]
    for load in loads:
        load.start()
    greet([peer, (left, head), (right, head)])

    def side_rows(side, c):
        return pl.ds(pl.multiple_of(side * count + head * count + c * step, step), step)

    def across(c, side):
        return pltpu.make_async_remote_copy(
            src_ref=rows.at[pl.ds(pl.multiple_of(c * step, step), step)], dst_ref=near.at[side_rows(side, c)],
            send_sem=send_sem.at[2 * c + side // 4], recv_sem=recv_sem.at[2 * c + side // 4],
            device_id=(left if side else right, head), device_id_type=MESH)

    def passed(c, side):
        ours = near.at[side_rows(side, c)]
        n = 2 * c + side // 4 + 2 * chunks
        return pltpu.make_async_remote_copy(
            src_ref=ours, dst_ref=ours, send_sem=send_sem.at[n], recv_sem=recv_sem.at[n],
            device_id=peer, device_id_type=MESH)

    mine = pl.ds(pl.multiple_of(2 * count + head * count, count), count)
    local = [pltpu.make_async_remote_copy(
        src_ref=src, dst_ref=dst, send_sem=send_sem.at[4 * chunks + n], recv_sem=recv_sem.at[4 * chunks + n],
        device_id=peer, device_id_type=MESH)
        for n, (src, dst) in enumerate(((wk, half_of(hold_k, 1, head)), (wv, half_of(hold_v, 1, head)), (rows, near.at[mine])))]
    for c in range(chunks):
        for side in (0, 4):
            across(c, side).start()
    for copy in local:
        copy.start()
    near[mine, :] = rows[...]
    for load in loads:
        load.wait()
    for copy in local:
        copy.wait_recv()

    def stores(base, slot):
        return [pltpu.make_async_copy(
            blocks.at[slot, kind, pl.ds(half * step, step)],
            table.at[pl.ds(pl.multiple_of(kind * (6 * count) + base + half * count, step), step)],
            store_sem.at[slot, 2 * kind + half]) for kind in range(2) for half in range(2)]

    def project_block(base, turn):
        slot = lax.rem(turn, 2)

        @pl.when(turn >= 2)
        def _():
            for store in stores(base, slot):
                store.wait()

        pieces = [pl.multiple_of(base + part * count, step) for part in range(2)]
        xf = jnp.concatenate([near[pl.ds(p, step), :] for p in pieces], axis=0).astype(jnp.float32)
        cen = xf - jnp.mean(xf, axis=-1, keepdims=True)
        var = jnp.mean(cen * cen, axis=-1, keepdims=True)
        xn = (cen * lax.rsqrt(var + EPSILON)).astype(jnp.bfloat16)
        for part, w in enumerate((hold_k, hold_k, hold_v, hold_v)):
            kv = jnp.dot(xn, w[:, part % 2 * 512:part % 2 * 512 + 512], preferred_element_type=jnp.float32)
            for s in range(4):
                at = part // 2 * (2 * step * 8) + part % 2 * 4 + s
                lines[pl.ds(slot * (4 * step * 8) + at, 2 * step, stride=8), :] = kv[:, s * 128:(s + 1) * 128]
        for store in stores(base, slot):
            store.start()

    def own(c, carry):
        project_block(2 * count + c * step, c)
        return carry

    lax.fori_loop(0, chunks, own, 0)
    out[...] = near[2 * count:4 * count, pl.ds(pl.multiple_of(head * (width // 2), width // 2), width // 2)]

    def waves(c, carry):
        for side in (0, 4):
            across(c, side).wait_recv()
            passed(c, side).start()
        for side in (0, 4):
            passed(c, side).wait_recv()
            project_block(side * count + c * step, chunks + 2 * c + side // 4)
        return carry

    lax.fori_loop(0, chunks, waves, 0)
    for slot in range(2):
        for store in stores(0, slot):
            store.wait()
    for c in range(chunks):
        for side in (0, 4):
            across(c, side).wait_send()
            passed(c, side).wait_send()
    for copy in local:
        copy.wait_send()


def final_tables(rows, wk, wv):
    count, width = rows.shape
    whole = (wk.shape[0], 2 * wk.shape[1])
    return pl.pallas_call(
        tables_kernel,
        out_shape=[jax.ShapeDtypeStruct((12 * count, 8, 128), jnp.float32), jax.ShapeDtypeStruct((2 * count, width // 2), rows.dtype)],
        in_specs=[VM, ANY, ANY],
        out_specs=[ANY, VM],
        scratch_shapes=[
            pltpu.VMEM((6 * count, width), rows.dtype),
            pltpu.VMEM(whole, wk.dtype),
            pltpu.VMEM(whole, wv.dtype),
            pltpu.VMEM((2, 2, count // 2, 8, 128), jnp.float32),
            pltpu.SemaphoreType.DMA((19,)),
            pltpu.SemaphoreType.DMA((19,)),
            pltpu.SemaphoreType.DMA((2,)),
            pltpu.SemaphoreType.DMA((2, 4))],
        compiler_params=pltpu.CompilerParams(collective_id=2, has_side_effects=True, vmem_limit_bytes=60 << 20),
        name="final_tables",
    )(rows, wk, wv)


E_ENC = 32
E_DEC = 4


def enc_kernel(idx, q, wk, wv, go, near, bias, out, table, g, qk, mg):
    i = pl.program_id(0)
    steps = pl.num_programs(0)
    nodes = q.shape[0]
    heads2 = q.shape[1] // 128
    lane = lax.broadcasted_iota(jnp.int32, (1, 128), 1)
    low = lane < 64

    @pl.when(i == 0)
    def _():
        band = go.shape[0]
        for part, ref in enumerate((near.at[0:band], go, near.at[band:])):
            @pl.loop(0, band // 128)
            def _(b):
                r = pl.multiple_of(b * 128, 128)
                table[pl.ds(part * band + r, 128), 0, :] = ref[pl.ds(r, 128), :].astype(jnp.float32)
        for c in range(heads2):
            qc = q[:, c * 128:(c + 1) * 128].astype(jnp.float32)
            wc = wk[:, c * 128:(c + 1) * 128]
            for par in range(2):
                qm = jnp.where(low if par == 0 else ~low, qc, 0.0).astype(jnp.bfloat16)
                r = lax.dot_general(qm, wc, (((1,), (1,)), ((), ())), preferred_element_type=jnp.float32)
                qk[2 * c + par] = (r * SCALE).astype(jnp.bfloat16)

    rows = NB * E_ENC
    for r in range(rows):
        g[r:r + 1, :] = table[idx[i * rows + r]]
    gb = g[...].astype(jnp.bfloat16)
    n0 = pl.multiple_of(i * NB, NB)
    qb = qk[:, pl.ds(n0, NB), :].reshape(heads2 * 2 * NB, 128)
    s = lax.dot_general(qb, gb, (((1,), (1,)), ((), ())), preferred_element_type=jnp.float32)
    rn = lax.broadcasted_iota(jnp.int32, s.shape, 0) % NB
    cn = lax.broadcasted_iota(jnp.int32, s.shape, 1) // E_ENC
    s = jnp.where(rn == cn, s + bias[0], NEGATIVE)
    p = jnp.exp(s)
    l = jnp.sum(p, axis=-1, keepdims=True)
    m = jnp.dot(p.astype(jnp.bfloat16), gb, preferred_element_type=jnp.float32) / l
    mg[:, pl.ds(n0, NB), :] = m.astype(jnp.bfloat16).reshape(heads2 * 2, NB, 128)

    @pl.when(i == steps - 1)
    def _():
        for c in range(heads2):
            wc = wv[:, c * 128:(c + 1) * 128]
            a = jnp.dot(mg[2 * c], wc, preferred_element_type=jnp.float32)
            b = jnp.dot(mg[2 * c + 1], wc, preferred_element_type=jnp.float32)
            out[:, c * 128:(c + 1) * 128] = jnp.where(low, a, b).astype(jnp.bfloat16)

def enc_attention(q, wk, wv, go, near, sources, counts):
    nodes, width = q.shape
    slots = sources.shape[1]
    steps = nodes // NB
    live = jnp.arange(slots, dtype=jnp.int32)[None, :] < counts[:, None]
    bias = jnp.where(live, 0.0, NEGATIVE).astype(jnp.float32).reshape(steps, 1, NB * slots)
    full = lambda a: pl.BlockSpec(a.shape, lambda i, s: (0,) * a.ndim, pipeline_mode=pl.Buffered(1))
    return pl.pallas_call(
        enc_kernel,
        out_shape=jax.ShapeDtypeStruct((nodes, width), jnp.bfloat16),
        grid_spec=pltpu.PrefetchScalarGridSpec(
            num_scalar_prefetch=1, grid=(steps,),
            in_specs=[full(q), full(wk), full(wv), full(go), full(near),
                      pl.BlockSpec((1, 1, NB * slots), lambda i, s: (i, 0, 0))],
            out_specs=pl.BlockSpec((nodes, width), lambda i, s: (0, 0)),
            scratch_shapes=[
                pltpu.VMEM((3 * go.shape[0], 1, 128), jnp.float32),
                pltpu.VMEM((NB * slots, 128), jnp.float32),
                pltpu.VMEM((width // 64, nodes, 128), jnp.bfloat16),
                pltpu.VMEM((width // 64, nodes, 128), jnp.bfloat16)]),
        compiler_params=pltpu.CompilerParams(dimension_semantics=("arbitrary",), vmem_limit_bytes=48 << 20),
        cost_estimate=pl.CostEstimate(flops=4 << 30, bytes_accessed=8 << 20, transcendentals=4 << 20),
        name="enc_attention",
    )(sources.reshape(-1), q, wk, wv, go, near, bias)


def win_kernel(q, k, v, ones, out, p):
    nodes = q.shape[0]
    span = p.shape[-1]
    lane = lax.broadcasted_iota(jnp.int32, (1, 128), 1)
    low = lane < 64
    for b in range(nodes // QB):
        s0 = b * QB
        kb = k[s0:s0 + span, :]
        ve = jnp.concatenate((v[s0:s0 + span, :], ones[s0:s0 + span, :]), axis=1)
        qc = q[s0:s0 + QB, :].astype(jnp.float32) * SCALE
        res = []
        for par in range(2):
            qm = jnp.where(low if par == 0 else ~low, qc, 0.0).astype(jnp.bfloat16)
            for t in range(0, span, 256):
                w = min(256, span - t)
                s = lax.dot_general(qm, kb[t:t + w, :], (((1,), (1,)), ((), ())), preferred_element_type=jnp.float32)
                e = jnp.exp(s)
                if t < QB or t + w - 1 > 2 * HALF_WIN:
                    d = lax.broadcasted_iota(jnp.int32, s.shape, 1) + t - lax.broadcasted_iota(jnp.int32, s.shape, 0)
                    e = jnp.where((d >= 0) & (d <= 2 * HALF_WIN), e, 0.0)
                p[2*b+par, :, t:t + w] = e.astype(jnp.bfloat16)
            o = jnp.dot(p[2*b+par], ve, preferred_element_type=jnp.float32)
            res.append(o[:, :128] / o[:, 128:])
        out[s0:s0 + QB, :] = jnp.where(low, res[0], res[1]).astype(jnp.bfloat16)

def window(q, k, v, ones):
    nodes, width = q.shape
    span = -(-(QB + 2 * HALF_WIN) // 128) * 128
    keys = k.shape[0]
    return pl.pallas_call(
        win_kernel, out_shape=jax.ShapeDtypeStruct((nodes, width), jnp.bfloat16),
        grid=(width // 128,),
        in_specs=[pl.BlockSpec((nodes, 128), lambda c: (0, c)), pl.BlockSpec((keys, 128), lambda c: (0, c)),
                  pl.BlockSpec((keys, 128), lambda c: (0, c)), pl.BlockSpec((keys, 128), lambda c: (0, 0))],
        out_specs=pl.BlockSpec((nodes, 128), lambda c: (0, c)),
        scratch_shapes=[pltpu.VMEM((2*nodes//QB, QB, span), jnp.bfloat16)],
        compiler_params=pltpu.CompilerParams(dimension_semantics=("arbitrary",), vmem_limit_bytes=48 << 20),
        name="window_attention")(q, k, v, ones)


def dec_kernel(idx, table, cnt, gs, wq, wo, out, q3, prod_a, held_a, prod_b, held_b, mix3, seg, live):
    i = pl.program_id(0)
    rows = table.shape[0] // 2
    lines = table.reshape(table.shape[0] * 8, 128)
    qlines = q3.reshape(GB * 8, 128)
    lives = live.reshape(E_DEC * GB, 128)
    mlines = mix3.reshape(GB * 8, 128)
    lane = lax.broadcasted_iota(jnp.int32, (1, 128), 1)

    @pl.when(i == 0)
    def _():
        r = lax.broadcasted_iota(jnp.int32, (128, 128), 0) // 64
        c = lax.broadcasted_iota(jnp.int32, (128, 128), 1) // 64
        seg[...] = jnp.where(r == c, 1.0, 0.0).astype(jnp.bfloat16)

    def work():
        g0 = i * GB
        gb = gs[...]
        qf = jnp.dot(gb, wq[...], preferred_element_type=jnp.float32) * (SCALE * LOG2E)
        for s in range(8):
            q3[:, s] = qf[:, s * 128:(s + 1) * 128].reshape(GB // 8, 8, 128)
        for e in range(E_DEC):
            live[e] = jnp.broadcast_to(jnp.where(cnt[...] > e, 1.0, 0.0), (GB, 128))

        def gather(o, prod, held):
            base = (g0 + o * UN) * E_DEC
            for j in range(UN):
                place = (j // 8) * 64 + j % 8
                qv = qlines[pl.ds(pl.multiple_of(o * (UN * 8), 64) + place, 8, stride=8), :]
                parts = []
                for e in range(E_DEC):
                    at = pl.multiple_of(idx[base + (j * E_DEC + e)], 8)
                    parts.append(qv * lines[pl.ds(at, 8), :])
                    held[j, e] = lines[pl.ds(at + rows * 8, 8), :]
                for h in range(E_DEC // 2):
                    prod[j, h] = jnp.concatenate(parts[2 * h:2 * h + 2], axis=0).astype(jnp.bfloat16)

        def mixing(o, prod, held):
            pm = prod[...].reshape(E_DEC * UN * 8, 128)
            sc = jnp.dot(pm, seg[...], preferred_element_type=jnp.float32).reshape(UN, E_DEC, 8, 128)
            for j in range(UN):
                tot = None
                for e in range(E_DEC):
                    pe = jnp.exp2(sc[j, e])
                    if e > 0:
                        pe = pe * lives[pl.ds(e * GB + (o * UN + j), 8, stride=0), :]
                    pv = pe * held[j, e]
                    tot = pe if e == 0 else tot + pe
                    acc = pv if e == 0 else acc + pv
                place = (j // 8) * 64 + j % 8
                mlines[pl.ds(pl.multiple_of(o * (UN * 8), 64) + place, 8, stride=8), :] = acc / tot

        rounds = GB // UN
        gather(0, prod_a, held_a)

        def both(o, carry):
            gather(2 * o + 1, prod_b, held_b)
            mixing(2 * o, prod_a, held_a)
            gather(2 * o + 2, prod_a, held_a)
            mixing(2 * o + 1, prod_b, held_b)
            return carry

        lax.fori_loop(0, rounds // 2 - 1, both, 0)
        gather(rounds - 1, prod_b, held_b)
        mixing(rounds - 2, prod_a, held_a)
        mixing(rounds - 1, prod_b, held_b)
        o = gb.astype(jnp.float32)
        m2 = jnp.concatenate([mix3[:, s].reshape(GB, 128) for s in range(8)], axis=1).astype(jnp.bfloat16)
        o = o + jnp.dot(m2, wo[...], preferred_element_type=jnp.float32)
        out[...] = o[:, :out.shape[1]].astype(jnp.bfloat16)

    work()

def decode(table, gs, wq, wo, sources, counts, variables):
    grid_rows = gs.shape[0]
    steps = grid_rows // GB
    full = lambda a: pl.BlockSpec(a.shape, lambda i, *_: (0,) * a.ndim, pipeline_mode=pl.Buffered(1))
    late = lambda i, *_: (i, 0)
    return pl.pallas_call(
        dec_kernel,
        out_shape=jax.ShapeDtypeStruct((grid_rows, variables), jnp.bfloat16),
        grid_spec=pltpu.PrefetchScalarGridSpec(
            num_scalar_prefetch=1, grid=(steps,),
            in_specs=[full(table),
                      pl.BlockSpec((GB, 1), late), pl.BlockSpec((GB, 128), late), full(wq), full(wo)],
            out_specs=pl.BlockSpec((GB, variables), late),
            scratch_shapes=[
                pltpu.VMEM((GB // 8, 8, 8, 128), jnp.float32),
                pltpu.VMEM((UN, E_DEC // 2, 16, 128), jnp.bfloat16),
                pltpu.VMEM((UN, E_DEC, 8, 128), jnp.float32),
                pltpu.VMEM((UN, E_DEC // 2, 16, 128), jnp.bfloat16),
                pltpu.VMEM((UN, E_DEC, 8, 128), jnp.float32),
                pltpu.VMEM((GB // 8, 8, 8, 128), jnp.float32),
                pltpu.VMEM((128, 128), jnp.bfloat16),
                pltpu.VMEM((E_DEC, GB, 128), jnp.float32)]),
        compiler_params=pltpu.CompilerParams(dimension_semantics=("arbitrary",), vmem_limit_bytes=60 << 20),
        name="dec_attention",
    )((sources * 8).reshape(-1), table, counts[:, None], gs, wq, wo)


def local(
    grid_state,
    hidden_state,
    encoder_sources,
    encoder_counts,
    decoder_sources,
    decoder_counts,
    encoder_keys,
    encoder_values,
    encoder_query,
    encoder_output,
    window_query,
    window_keys,
    window_values,
    window_output,
    feed_up,
    feed_down,
    decoder_query,
    decoder_keys,
    decoder_values,
    decoder_output,
):
    band, head, _, _ = places()
    bands = lax.axis_size("band")
    band_nodes, half_width = hidden_state.shape
    nodes = band_nodes // 2
    grid_count, variables = grid_state.shape
    half_grid = grid_count // 2
    short = 128 - variables
    widen = lambda w: jnp.pad(w, ((0, short), (0, 0)))
    grid = jnp.pad(grid_state, ((0, 0), (0, short)))
    near_grid, state, enc_k, enc_v, enc_q, enc_o, win_q, win_k, win_v, win_o, dec_q, dec_o = start_exchange(
        grid, hidden_state,
        [(widen(encoder_keys), 1), (widen(encoder_values), 1), (encoder_query, 1), (encoder_output, 0),
         (window_query, 1), (window_keys, 1), (window_values, 1), (window_output, 0),
         (widen(decoder_query), 1), (jnp.pad(decoder_output, ((0, 0), (0, short))), 0)],
    )
    my_rows = lambda a, size: lax.dynamic_slice_in_dim(a, head * size, size, 0)
    query = project(layer_norm(state), enc_q)
    mix = enc_attention(query, enc_k, enc_v, grid, near_grid, my_rows(encoder_sources, nodes), my_rows(encoder_counts, nodes))
    mid = (state.astype(jnp.float32) + jnp.dot(mix, enc_o, preferred_element_type=jnp.float32)).astype(jnp.bfloat16)
    normed = layer_norm(mid)
    span = nodes + 2 * HALF_WIN
    span_rows = nodes - QB + -(-(QB + 2 * HALF_WIN) // 128) * 128
    query, keys, values, up, down = window_span(normed, span_rows, win_q, win_k, win_v, [(feed_up, 1), (feed_down, 0)])
    place = jnp.arange(span_rows, dtype=jnp.int32)
    node = band * band_nodes + head * nodes - HALF_WIN + place
    live = ((place < span) & (node >= 0) & (node < bands * band_nodes))[:, None]
    ones = jnp.broadcast_to(live, (span_rows, 128)).astype(jnp.bfloat16)
    mixed = window(query, keys, values, ones)
    att = (mid.astype(jnp.float32) + jnp.dot(mixed, win_o, preferred_element_type=jnp.float32)).astype(jnp.bfloat16)
    inner = jax.nn.gelu(
        jnp.dot(layer_norm(att), up, preferred_element_type=jnp.float32), approximate=True
    ).astype(jnp.bfloat16)
    final = (att.astype(jnp.float32) + jnp.dot(inner, down, preferred_element_type=jnp.float32)).astype(jnp.bfloat16)
    table, hidden_final = final_tables(final, decoder_keys, decoder_values)
    sources = my_rows(decoder_sources, half_grid) - (band - 1) * band_nodes
    grid_next = decode(table, my_rows(grid, half_grid), dec_q, dec_o, sources,
                       my_rows(decoder_counts, half_grid), variables)
    return (grid_next, hidden_final)


def solution(mesh):
    in_specs = (
        P("band", None),
        P("band", "head"),
        P("band", None),
        P("band"),
        P("band", None),
        P("band"),
        P(None, "head"),
        P(None, "head"),
        P(None, "head"),
        P("head", None),
        P(None, "head"),
        P(None, "head"),
        P(None, "head"),
        P("head", None),
        P(None, "head"),
        P("head", None),
        P(None, "head"),
        P(None, "head"),
        P(None, "head"),
        P("head", None),
    )
    out_specs = (P(("band", "head"), None), P("band", "head"))
    return jax.shard_map(local, mesh=mesh, in_specs=in_specs, out_specs=out_specs, check_vma=False)
```

```python
import functools

import jax
import jax.numpy as jnp
from jax import lax
from jax.experimental import pallas as pl
from jax.experimental.pallas import tpu as pltpu
from jax.sharding import PartitionSpec as P

HALF_WIN = 560
HEAD_DIM = 64
EPSILON = 1e-05
NEGATIVE = -1e30
SCALE = HEAD_DIM**-0.5
LOG2E = 1.4426950408889634
MESH = pl.DeviceIdType.MESH
NB = 16
QB = 128
GB = 128
UN = 16
ANY = pl.BlockSpec(memory_space=pltpu.HBM)
VM = pl.BlockSpec(memory_space=pltpu.VMEM)


def layer_norm(matrix):
    as_float = matrix.astype(jnp.float32)
    centred = as_float - jnp.mean(as_float, axis=-1, keepdims=True)
    variance = jnp.mean(centred * centred, axis=-1, keepdims=True)
    return (centred * lax.rsqrt(variance + EPSILON)).astype(jnp.bfloat16)


def project(matrix, weight):
    return jnp.dot(matrix, weight, preferred_element_type=jnp.float32).astype(jnp.bfloat16)


def places():
    band = lax.axis_index("band")
    head = lax.axis_index("head")
    count = lax.axis_size("band")
    left = lax.rem(band + count - 1, count)
    right = lax.rem(band + 1, count)
    return band, head, left, right


def greet(others):
    barrier = pltpu.get_barrier_semaphore()
    for other in others:
        pl.semaphore_signal(barrier, inc=1, device_id=other, device_id_type=MESH)
    pl.semaphore_wait(barrier, len(others))


class Sender:
    def __init__(self, send_sem, recv_sem):
        self.send_sem, self.recv_sem, self.used, self.open = send_sem, recv_sem, 0, []

    def send(self, src, dst, device):
        n = self.used
        self.used += 1
        copy = pltpu.make_async_remote_copy(
            src_ref=src, dst_ref=dst, send_sem=self.send_sem.at[n], recv_sem=self.recv_sem.at[n],
            device_id=device, device_id_type=MESH)
        copy.start()
        self.open.append(copy)
        return copy

    def finish(self, received=()):
        for copy in self.open:
            copy.wait_send()
            if not any(copy is other for other in received):
                copy.wait_recv()


def half_of(ref, dim, index):
    size = ref.shape[dim] // 2
    part = pl.ds(pl.multiple_of(index * size, size), size)
    return ref.at[part] if dim == 0 else ref.at[:, part]


def relay(near, source, width, sides, sender, me, band, left, right, head, chunks):
    step = width // 2 // chunks
    waves = []
    for c in range(chunks):
        own = pl.ds(pl.multiple_of(head * (width // 2) + c * step, step), step)
        for side, other in ((sides[0], right), (sides[1], left)):
            rows = pl.ds(pl.multiple_of(side * width + head * (width // 2) + c * step, step), step)
            waves.append((sender.send(source(own, c, step), near.at[rows], (other, head)), rows))
    return waves


def start_kernel(n_pair, dims, *refs):
    grid, state, wq = refs[:3]
    halves = refs[3 : 3 + n_pair]
    near, whole_out, query = refs[3 + n_pair : 6 + n_pair]
    fulls = refs[6 + n_pair : 6 + 2 * n_pair]
    rest = refs[6 + 2 * n_pair :]
    whole, hold_q = rest[:2]
    holds = rest[2 : 2 + n_pair]
    send_sem, recv_sem, load_sem, store_sem = rest[2 + n_pair :]
    band, head, left, right = places()
    peer = (band, 1 - head)
    early = [pltpu.make_async_copy(half_of(state, 0, head), half_of(whole, 1, head), load_sem.at[n_pair]),
             pltpu.make_async_copy(wq, half_of(hold_q, 1, head), load_sem.at[n_pair + 1])]
    loads = [pltpu.make_async_copy(h, v, load_sem.at[n]) for n, (h, v) in enumerate(zip(halves, holds))]
    for load in early + loads:
        load.start()
    greet([peer, (left, head), (right, head)])
    sender = Sender(send_sem, recv_sem)
    waves = relay(near, lambda own, c, step: grid.at[own], grid.shape[0], (0, 1), sender, None, band, left, right, head, 4)
    first = [sender.send(half_of(state, 0, 1 - head), half_of(whole, 1, head), peer),
             sender.send(wq, half_of(hold_q, 1, head), peer)]
    for n in range(n_pair):
        sender.send(halves[n], half_of(fulls[n], dims[n], head), peer)
    stores = [pltpu.make_async_copy(holds[n], half_of(fulls[n], dims[n], head), store_sem.at[n]) for n in range(n_pair)]
    for load, store in zip(loads, stores):
        load.wait()
        store.start()
    for load in early:
        load.wait()
    for copy in first:
        copy.wait_recv()
    block = whole.shape[0] // 2
    for b in range(2):
        x = whole[b * block:(b + 1) * block, :]
        whole_out[b * block:(b + 1) * block, :] = x
        query[b * block:(b + 1) * block, :] = project(layer_norm(x), hold_q[...])
    for copy, rows in waves:
        copy.wait_recv()
        sender.send(near.at[rows], near.at[rows], peer)
    sender.finish([copy for copy, _ in waves] + first)
    for store in stores:
        store.wait()


def full_shape(half, dim):
    shape = list(half.shape)
    shape[dim] *= 2
    return jax.ShapeDtypeStruct(tuple(shape), half.dtype)


def start_exchange(grid, state, wq, pairs):
    halves = [half for half, _ in pairs]
    dims = [dim for _, dim in pairs]
    n = len(pairs)
    nodes, width = state.shape
    rows = jax.ShapeDtypeStruct((nodes // 2, width * 2), state.dtype)
    outs = [jax.ShapeDtypeStruct((2 * grid.shape[0], grid.shape[1]), grid.dtype), rows, rows]
    outs += [full_shape(half, dim) for half, dim in pairs]
    copies = 16 + 2 + n
    return pl.pallas_call(
        functools.partial(start_kernel, n, dims),
        out_shape=outs,
        in_specs=[VM] + [ANY] * (n + 2),
        out_specs=[ANY, VM, VM] + [ANY] * n,
        scratch_shapes=[pltpu.VMEM(rows.shape, state.dtype), pltpu.VMEM(full_shape(wq, 1).shape, wq.dtype)]
        + [pltpu.VMEM(half.shape, half.dtype) for half in halves]
        + [pltpu.SemaphoreType.DMA((copies,))] * 2
        + [pltpu.SemaphoreType.DMA((n + 2,)), pltpu.SemaphoreType.DMA((n,))],
        compiler_params=pltpu.CompilerParams(collective_id=0, has_side_effects=True, vmem_limit_bytes=60 << 20),
        name="start_exchange",
    )(grid, state, wq, *halves)


def span_kernel(n_pair, dims, *refs):
    rows, wq, wk, wv = refs[:4]
    halves = refs[4 : 4 + n_pair]
    q, k, v = refs[4 + n_pair : 7 + n_pair]
    fulls = refs[7 + n_pair : 7 + 2 * n_pair]
    span, hold_q, hold_k, hold_v = refs[7 + 2 * n_pair : 11 + 2 * n_pair]
    holds = refs[11 + 2 * n_pair : 11 + 3 * n_pair]
    send_sem, recv_sem, load_sem, store_sem = refs[11 + 3 * n_pair :]
    band, head, left, right = places()
    bands = lax.axis_size("band")
    count, width = rows.shape
    extra = HALF_WIN - count
    after = HALF_WIN + count
    chunks = 4
    step = count // chunks
    peer = (band, 1 - head)
    beside = (lax.rem(band + bands + 2 * head - 1, bands), 1 - head)
    weights = [pltpu.make_async_copy(w, hold, load_sem.at[n_pair + n]) for n, (w, hold) in enumerate(((wq, hold_q), (wk, hold_k), (wv, hold_v)))]
    for load in weights:
        load.start()
    loads = [pltpu.make_async_copy(h, hold, load_sem.at[n]) for n, (h, hold) in enumerate(zip(halves, holds))]
    for load in loads:
        load.start()
    greet([peer, (left, head), (right, head), beside])
    sender = Sender(send_sem, recv_sem)
    from_beside = extra + head * (after - extra)
    from_peer = after + head * (extra - after)
    first = sender.send(rows.at[pl.ds(count - extra, extra)], span.at[pl.ds(0, extra)], (right, head))
    last = sender.send(rows.at[pl.ds(0, extra)], span.at[pl.ds(after + count, extra)], (left, head))
    waves = [sender.send(rows.at[pl.ds(c * step, step)], span.at[pl.ds(pl.multiple_of(from_peer + c * step, 16), step)], beside)
             for c in range(chunks)]
    partner = sender.send(rows, span.at[pl.ds(pl.multiple_of(from_beside, 16), count)], peer)
    for n in range(n_pair):
        sender.send(halves[n], half_of(fulls[n], dims[n], head), peer)
    for load in weights:
        load.wait()

    def pair(x, place, size):
        node = band * (2 * count) + head * count - HALF_WIN + place + lax.broadcasted_iota(jnp.int32, (size, 1), 0)
        live = (node >= 0) & (node < bands * 2 * count)
        for w, o in ((hold_k, k), (hold_v, v)):
            o[pl.ds(place, size), :] = jnp.where(live, jnp.dot(x, w[...], preferred_element_type=jnp.float32), 0.0).astype(jnp.bfloat16)

    half = count // 2
    for b in range(2):
        x = rows[b * half:(b + 1) * half, :]
        q[b * half:(b + 1) * half, :] = jnp.dot(x, hold_q[...], preferred_element_type=jnp.float32).astype(jnp.bfloat16)
        pair(x, HALF_WIN + b * half, half)
    stores = [pltpu.make_async_copy(holds[n], half_of(fulls[n], dims[n], head), store_sem.at[n]) for n in range(n_pair)]
    for load, store in zip(loads, stores):
        load.wait()
        store.start()
    partner.wait_recv()
    for b in range(2):
        place = pl.multiple_of(from_peer + b * half, 16)
        pair(span[pl.ds(place, half), :], place, half)
    first.wait_recv()
    last.wait_recv()
    tail = span.shape[0] - after - count - extra
    pad = jnp.zeros((tail, width), rows.dtype)
    pair(span[0:extra, :], 0, extra)
    pair(jnp.concatenate((span[after + count:after + count + extra, :], pad), axis=0), after + count, extra + tail)
    for b in range(2):
        for c in range(b * chunks // 2, (b + 1) * chunks // 2):
            waves[c].wait_recv()
        place = pl.multiple_of(from_beside + b * half, 16)
        pair(span[pl.ds(place, half), :], place, half)
    sender.finish(waves + [first, last, partner])
    for store in stores:
        store.wait()


def window_span(rows, span_rows, wq, wk, wv, pairs):
    halves = [half for half, _ in pairs]
    dims = [dim for _, dim in pairs]
    n = len(pairs)
    outs = [jax.ShapeDtypeStruct((size, rows.shape[1]), rows.dtype) for size in (rows.shape[0], span_rows, span_rows)]
    outs += [full_shape(half, dim) for half, dim in pairs]
    copies = 7 + n
    return pl.pallas_call(
        functools.partial(span_kernel, n, dims),
        out_shape=outs,
        in_specs=[VM] + [ANY] * (n + 3),
        out_specs=[VM] * 3 + [ANY] * n,
        scratch_shapes=[pltpu.VMEM((span_rows, rows.shape[1]), rows.dtype)]
        + [pltpu.VMEM(w.shape, w.dtype) for w in (wq, wk, wv)]
        + [pltpu.VMEM(half.shape, half.dtype) for half in halves]
        + [pltpu.SemaphoreType.DMA((copies,))] * 2
        + [pltpu.SemaphoreType.DMA((n + 3,)), pltpu.SemaphoreType.DMA((n,))],
        compiler_params=pltpu.CompilerParams(collective_id=1, has_side_effects=True, vmem_limit_bytes=46 << 20),
        name="window_span",
    )(rows, wq, wk, wv, *halves)


def tables_kernel(att, up, down, wk, wv, table, out, rows, inner, near, hold_u, hold_d, hold_k, hold_v, blocks,
                  send_sem, recv_sem, load_sem, store_sem):
    band, head, left, right = places()
    count, width = rows.shape
    chunks = 4
    step = count // chunks
    block = count // 2
    peer = (band, 1 - head)
    lines = blocks.reshape(blocks.shape[0] * blocks.shape[1] * blocks.shape[2] * 8, 128)
    feeds = [pltpu.make_async_copy(up, hold_u, load_sem.at[2]), pltpu.make_async_copy(down, hold_d, load_sem.at[3])]
    loads = [pltpu.make_async_copy(half, half_of(hold, 1, head), load_sem.at[n])
             for n, (half, hold) in enumerate(((wk, hold_k), (wv, hold_v)))]
    for load in feeds + loads:
        load.start()
    greet([peer, (left, head), (right, head)])

    def side_rows(side, c):
        return pl.ds(pl.multiple_of(side * count + head * count + c * step, step), step)

    def across(c, side):
        return pltpu.make_async_remote_copy(
            src_ref=rows.at[pl.ds(pl.multiple_of(c * step, step), step)], dst_ref=near.at[side_rows(side, c)],
            send_sem=send_sem.at[2 * c + side // 4], recv_sem=recv_sem.at[2 * c + side // 4],
            device_id=(left if side else right, head), device_id_type=MESH)

    def passed(c, side):
        ours = near.at[side_rows(side, c)]
        n = 2 * c + side // 4 + 2 * chunks
        return pltpu.make_async_remote_copy(
            src_ref=ours, dst_ref=ours, send_sem=send_sem.at[n], recv_sem=recv_sem.at[n],
            device_id=peer, device_id_type=MESH)

    base = 2 * count + head * count
    mine = [pl.ds(pl.multiple_of(base + h * block, block), block) for h in range(2)]
    local = [pltpu.make_async_remote_copy(
        src_ref=src, dst_ref=dst, send_sem=send_sem.at[4 * chunks + n], recv_sem=recv_sem.at[4 * chunks + n],
        device_id=peer, device_id_type=MESH)
        for n, (src, dst) in enumerate(((wk, half_of(hold_k, 1, head)), (wv, half_of(hold_v, 1, head)),
                                        (rows.at[0:block], near.at[mine[0]]), (rows.at[block:], near.at[mine[1]])))]
    for copy in local[:2]:
        copy.start()

    def send_half(h):
        for c in range(h * chunks // 2, (h + 1) * chunks // 2):
            for side in (0, 4):
                across(c, side).start()
        local[2 + h].start()

    feeds[0].wait()
    part = up.shape[1] // 8
    for h in range(2):
        x = att[h * block:(h + 1) * block, :]
        xn = layer_norm(x)
        if h == 1:
            send_half(0)

        def rise(n, carry):
            for m in range(2):
                cols = pl.ds(pl.multiple_of((2 * n + m) * part, part), part)
                up_rows = jnp.dot(xn, hold_u[:, cols], preferred_element_type=jnp.float32)
                inner[:, cols] = jax.nn.gelu(up_rows, approximate=True).astype(jnp.bfloat16)
            return carry

        lax.fori_loop(0, 4, rise, 0)
        if h == 0:
            feeds[1].wait()
        for n in range(2):
            cols = slice(n * width // 2, (n + 1) * width // 2)
            total = x[:, cols].astype(jnp.float32) + jnp.dot(inner[...], hold_d[:, cols], preferred_element_type=jnp.float32)
            total = total.astype(jnp.bfloat16)
            rows[h * block:(h + 1) * block, cols] = total
            near[mine[h], cols] = total

    def stores(base, slot):
        return [pltpu.make_async_copy(
            blocks.at[slot, kind, pl.ds(half * step, step)],
            table.at[pl.ds(pl.multiple_of(kind * (6 * count) + base + half * count, step), step)],
            store_sem.at[slot, 2 * kind + half]) for kind in range(2) for half in range(2)]

    def project_block(base, turn):
        slot = lax.rem(turn, 2)

        @pl.when(turn >= 2)
        def _():
            for store in stores(base, slot):
                store.wait()

        pieces = [pl.multiple_of(base + part * count, step) for part in range(2)]
        xf = jnp.concatenate([near[pl.ds(p, step), :] for p in pieces], axis=0).astype(jnp.float32)
        cen = xf - jnp.mean(xf, axis=-1, keepdims=True)
        var = jnp.mean(cen * cen, axis=-1, keepdims=True)
        xn = (cen * lax.rsqrt(var + EPSILON)).astype(jnp.bfloat16)
        for part, w in enumerate((hold_k, hold_k, hold_v, hold_v)):
            kv = jnp.dot(xn, w[:, part % 2 * 512:part % 2 * 512 + 512], preferred_element_type=jnp.float32)
            for s in range(4):
                at = part // 2 * (2 * step * 8) + part % 2 * 4 + s
                lines[pl.ds(slot * (4 * step * 8) + at, 2 * step, stride=8), :] = kv[:, s * 128:(s + 1) * 128]
        for store in stores(base, slot):
            store.start()

    for load in loads:
        load.wait()
    for copy in local[:2]:
        copy.wait_recv()

    def own(c, turn):
        project_block(2 * count + c * step, turn)
        return turn + 1

    def waves(c, turn):
        for side in (0, 4):
            across(c, side).wait_recv()
            passed(c, side).start()
        for side in (0, 4):
            passed(c, side).wait_recv()
            project_block(side * count + c * step, turn + side // 4)
        return turn + 2

    local[2].wait_recv()
    turn = lax.fori_loop(0, 2, own, 0)
    send_half(1)
    turn = lax.fori_loop(0, 2, waves, turn)
    local[3].wait_recv()
    turn = lax.fori_loop(2, 4, own, turn)
    out[...] = near[2 * count:4 * count, pl.ds(pl.multiple_of(head * (width // 2), width // 2), width // 2)]
    lax.fori_loop(2, 4, waves, turn)
    for slot in range(2):
        for store in stores(0, slot):
            store.wait()
    for c in range(chunks):
        for side in (0, 4):
            across(c, side).wait_send()
            passed(c, side).wait_send()
    for copy in local:
        copy.wait_send()


def final_tables(att, up, down, wk, wv):
    count, width = att.shape
    whole = (wk.shape[0], 2 * wk.shape[1])
    return pl.pallas_call(
        tables_kernel,
        out_shape=[jax.ShapeDtypeStruct((12 * count, 8, 128), jnp.float32), jax.ShapeDtypeStruct((2 * count, width // 2), att.dtype)],
        in_specs=[VM, ANY, ANY, ANY, ANY],
        out_specs=[ANY, VM],
        scratch_shapes=[
            pltpu.VMEM((count, width), att.dtype),
            pltpu.VMEM((count // 2, up.shape[1]), att.dtype),
            pltpu.VMEM((6 * count, width), att.dtype),
            pltpu.VMEM(up.shape, up.dtype),
            pltpu.VMEM(down.shape, down.dtype),
            pltpu.VMEM(whole, wk.dtype),
            pltpu.VMEM(whole, wv.dtype),
            pltpu.VMEM((2, 2, count // 2, 8, 128), jnp.float32),
            pltpu.SemaphoreType.DMA((20,)),
            pltpu.SemaphoreType.DMA((20,)),
            pltpu.SemaphoreType.DMA((4,)),
            pltpu.SemaphoreType.DMA((2, 4))],
        compiler_params=pltpu.CompilerParams(collective_id=2, has_side_effects=True, vmem_limit_bytes=60 << 20),
        name="final_tables",
    )(att, up, down, wk, wv)


E_ENC = 32
E_DEC = 4


def enc_kernel(idx, q, wk, wv, go, near, bias, out, table, g_a, g_b, qk, mg):
    i = pl.program_id(0)
    steps = pl.num_programs(0)
    nodes = q.shape[0]
    heads2 = q.shape[1] // 128
    lane = lax.broadcasted_iota(jnp.int32, (1, 128), 1)
    low = lane < 64

    @pl.when(i == 0)
    def _():
        band = go.shape[0]
        for part, ref in enumerate((near.at[0:band], go, near.at[band:])):
            @pl.loop(0, band // 128)
            def _(b):
                r = pl.multiple_of(b * 128, 128)
                table[pl.ds(part * band + r, 128), :] = ref[pl.ds(r, 128), :].astype(jnp.float32)
        for c in range(heads2):
            qc = q[:, c * 128:(c + 1) * 128].astype(jnp.float32)
            wc = wk[:, c * 128:(c + 1) * 128]
            for par in range(2):
                qm = jnp.where(low if par == 0 else ~low, qc, 0.0).astype(jnp.bfloat16)
                r = lax.dot_general(qm, wc, (((1,), (1,)), ((), ())), preferred_element_type=jnp.float32)
                qk[2 * c + par] = (r * SCALE).astype(jnp.bfloat16)

    rows = NB * E_ENC

    def gather(block, g):
        base = block * rows
        for r in range(rows):
            g[r:r + 1, :] = table[pl.ds(idx[base + r], 1), :]

    def mixing(block, g):
        gb = g[...].astype(jnp.bfloat16)
        n0 = pl.multiple_of(block * NB, NB)
        qb = qk[:, pl.ds(n0, NB), :].reshape(heads2 * 2 * NB, 128)
        s = lax.dot_general(qb, gb, (((1,), (1,)), ((), ())), preferred_element_type=jnp.float32)
        rn = lax.broadcasted_iota(jnp.int32, s.shape, 0) % NB
        cn = lax.broadcasted_iota(jnp.int32, s.shape, 1) // E_ENC
        s = jnp.where(rn == cn, s + bias[block], NEGATIVE)
        p = jnp.exp(s)
        l = jnp.sum(p, axis=-1, keepdims=True)
        m = jnp.dot(p.astype(jnp.bfloat16), gb, preferred_element_type=jnp.float32) / l
        mg[:, pl.ds(n0, NB), :] = m.astype(jnp.bfloat16).reshape(heads2 * 2, NB, 128)

    gather(2 * i, g_a)
    mixing(jnp.maximum(2 * i - 1, 0), g_b)
    gather(2 * i + 1, g_b)
    mixing(2 * i, g_a)

    @pl.when(i == steps - 1)
    def _():
        mixing(2 * i + 1, g_b)
        for c in range(heads2):
            wc = wv[:, c * 128:(c + 1) * 128]
            a = jnp.dot(mg[2 * c], wc, preferred_element_type=jnp.float32)
            b = jnp.dot(mg[2 * c + 1], wc, preferred_element_type=jnp.float32)
            out[:, c * 128:(c + 1) * 128] = jnp.where(low, a, b).astype(jnp.bfloat16)

def enc_attention(q, wk, wv, go, near, sources, counts):
    nodes, width = q.shape
    slots = sources.shape[1]
    steps = nodes // NB
    live = jnp.arange(slots, dtype=jnp.int32)[None, :] < counts[:, None]
    bias = jnp.where(live, 0.0, NEGATIVE).astype(jnp.float32).reshape(steps, 1, NB * slots)
    full = lambda a: pl.BlockSpec(a.shape, lambda i, s: (0,) * a.ndim, pipeline_mode=pl.Buffered(1))
    return pl.pallas_call(
        enc_kernel,
        out_shape=jax.ShapeDtypeStruct((nodes, width), jnp.bfloat16),
        grid_spec=pltpu.PrefetchScalarGridSpec(
            num_scalar_prefetch=1, grid=(steps // 2,),
            in_specs=[full(q), full(wk), full(wv), full(go), full(near),
                      full(bias)],
            out_specs=pl.BlockSpec((nodes, width), lambda i, s: (0, 0)),
            scratch_shapes=[
                pltpu.VMEM((3 * go.shape[0], 128), jnp.float32),
                pltpu.VMEM((NB * slots, 128), jnp.float32),
                pltpu.VMEM((NB * slots, 128), jnp.float32),
                pltpu.VMEM((width // 64, nodes, 128), jnp.bfloat16),
                pltpu.VMEM((width // 64, nodes, 128), jnp.bfloat16)]),
        compiler_params=pltpu.CompilerParams(dimension_semantics=("arbitrary",), vmem_limit_bytes=48 << 20),
        cost_estimate=pl.CostEstimate(flops=4 << 30, bytes_accessed=8 << 20, transcendentals=4 << 20),
        name="enc_attention",
    )(sources.reshape(-1), q, wk, wv, go, near, bias)


def win_kernel(q, k, v, ones, out, p):
    nodes = q.shape[0]
    span = p.shape[-1]
    lane = lax.broadcasted_iota(jnp.int32, (1, 128), 1)
    low = lane < 64
    for b in range(nodes // QB):
        s0 = b * QB
        kb = k[s0:s0 + span, :]
        ve = jnp.concatenate((v[s0:s0 + span, :], ones[s0:s0 + span, :]), axis=1)
        qc = q[s0:s0 + QB, :].astype(jnp.float32) * SCALE
        res = []
        for par in range(2):
            qm = jnp.where(low if par == 0 else ~low, qc, 0.0).astype(jnp.bfloat16)
            for t in range(0, span, 256):
                w = min(256, span - t)
                s = lax.dot_general(qm, kb[t:t + w, :], (((1,), (1,)), ((), ())), preferred_element_type=jnp.float32)
                e = jnp.exp(s)
                if t < QB or t + w - 1 > 2 * HALF_WIN:
                    d = lax.broadcasted_iota(jnp.int32, s.shape, 1) + t - lax.broadcasted_iota(jnp.int32, s.shape, 0)
                    e = jnp.where((d >= 0) & (d <= 2 * HALF_WIN), e, 0.0)
                p[2*b+par, :, t:t + w] = e.astype(jnp.bfloat16)
            o = jnp.dot(p[2*b+par], ve, preferred_element_type=jnp.float32)
            res.append(o[:, :128] / o[:, 128:])
        out[s0:s0 + QB, :] = jnp.where(low, res[0], res[1]).astype(jnp.bfloat16)

def window(q, k, v, ones):
    nodes, width = q.shape
    span = -(-(QB + 2 * HALF_WIN) // 128) * 128
    keys = k.shape[0]
    return pl.pallas_call(
        win_kernel, out_shape=jax.ShapeDtypeStruct((nodes, width), jnp.bfloat16),
        grid=(width // 128,),
        in_specs=[pl.BlockSpec((nodes, 128), lambda c: (0, c)), pl.BlockSpec((keys, 128), lambda c: (0, c)),
                  pl.BlockSpec((keys, 128), lambda c: (0, c)), pl.BlockSpec((keys, 128), lambda c: (0, 0))],
        out_specs=pl.BlockSpec((nodes, 128), lambda c: (0, c)),
        scratch_shapes=[pltpu.VMEM((2*nodes//QB, QB, span), jnp.bfloat16)],
        compiler_params=pltpu.CompilerParams(dimension_semantics=("arbitrary",), vmem_limit_bytes=48 << 20),
        name="window_attention")(q, k, v, ones)


def dec_kernel(idx, table, cnt, gs, wq, wo, out, q3, prod_a, held_a, prod_b, held_b, mix3, seg, live):
    i = pl.program_id(0)
    rows = table.shape[0] // 2
    lines = table.reshape(table.shape[0] * 8, 128)
    qlines = q3.reshape(GB * 8, 128)
    lives = live.reshape(E_DEC * GB, 128)
    mlines = mix3.reshape(GB * 8, 128)
    lane = lax.broadcasted_iota(jnp.int32, (1, 128), 1)

    @pl.when(i == 0)
    def _():
        r = lax.broadcasted_iota(jnp.int32, (128, 128), 0) // 64
        c = lax.broadcasted_iota(jnp.int32, (128, 128), 1) // 64
        seg[...] = jnp.where(r == c, 1.0, 0.0).astype(jnp.bfloat16)

    def work():
        g0 = i * GB
        gb = gs[...]
        qf = jnp.dot(gb, wq[...], preferred_element_type=jnp.float32) * (SCALE * LOG2E)
        for s in range(8):
            q3[:, s] = qf[:, s * 128:(s + 1) * 128].reshape(GB // 8, 8, 128)
        slots = jnp.broadcast_to(cnt[0].astype(jnp.float32), (128, GB)).T
        for e in range(E_DEC):
            live[e] = jnp.where(slots > e, 1.0, 0.0)

        def gather(o, prod, held):
            base = (g0 + o * UN) * E_DEC
            for j in range(UN):
                place = (j // 8) * 64 + j % 8
                qv = qlines[pl.ds(pl.multiple_of(o * (UN * 8), 64) + place, 8, stride=8), :]
                parts = []
                for e in range(E_DEC):
                    at = pl.multiple_of(idx[base + (j * E_DEC + e)], 8)
                    parts.append(qv * lines[pl.ds(at, 8), :])
                    held[j, e] = lines[pl.ds(at + rows * 8, 8), :]
                for h in range(E_DEC // 2):
                    prod[j, h] = jnp.concatenate(parts[2 * h:2 * h + 2], axis=0).astype(jnp.bfloat16)

        def mixing(o, prod, held):
            pm = prod[...].reshape(E_DEC * UN * 8, 128)
            sc = jnp.dot(pm, seg[...], preferred_element_type=jnp.float32).reshape(UN, E_DEC, 8, 128)
            for j in range(UN):
                tot = None
                for e in range(E_DEC):
                    pe = jnp.exp2(sc[j, e])
                    if e > 0:
                        pe = pe * lives[pl.ds(e * GB + (o * UN + j), 8, stride=0), :]
                    pv = pe * held[j, e]
                    tot = pe if e == 0 else tot + pe
                    acc = pv if e == 0 else acc + pv
                place = (j // 8) * 64 + j % 8
                mlines[pl.ds(pl.multiple_of(o * (UN * 8), 64) + place, 8, stride=8), :] = acc / tot

        rounds = GB // UN
        gather(0, prod_a, held_a)

        def both(o, carry):
            gather(2 * o + 1, prod_b, held_b)
            mixing(2 * o, prod_a, held_a)
            gather(2 * o + 2, prod_a, held_a)
            mixing(2 * o + 1, prod_b, held_b)
            return carry

        lax.fori_loop(0, rounds // 2 - 1, both, 0)
        gather(rounds - 1, prod_b, held_b)
        mixing(rounds - 2, prod_a, held_a)
        mixing(rounds - 1, prod_b, held_b)
        o = gb.astype(jnp.float32)
        m2 = jnp.concatenate([mix3[:, s].reshape(GB, 128) for s in range(8)], axis=1).astype(jnp.bfloat16)
        o = o + jnp.dot(m2, wo[...], preferred_element_type=jnp.float32)
        out[...] = o.T[:out.shape[0], :].astype(jnp.bfloat16)

    work()

def decode(table, gs, wq, wo, sources, counts, variables):
    grid_rows = gs.shape[0]
    steps = grid_rows // GB
    full = lambda a: pl.BlockSpec(a.shape, lambda i, *_: (0,) * a.ndim, pipeline_mode=pl.Buffered(1))
    late = lambda i, *_: (i, 0)
    return pl.pallas_call(
        dec_kernel,
        out_shape=jax.ShapeDtypeStruct((variables, grid_rows), jnp.bfloat16),
        grid_spec=pltpu.PrefetchScalarGridSpec(
            num_scalar_prefetch=1, grid=(steps,),
            in_specs=[full(table),
                      pl.BlockSpec((1, 1, GB), lambda i, *_: (i, 0, 0)), pl.BlockSpec((GB, 128), late), full(wq), full(wo)],
            out_specs=pl.BlockSpec((variables, GB), lambda i, *_: (0, i)),
            scratch_shapes=[
                pltpu.VMEM((GB // 8, 8, 8, 128), jnp.float32),
                pltpu.VMEM((UN, E_DEC // 2, 16, 128), jnp.bfloat16),
                pltpu.VMEM((UN, E_DEC, 8, 128), jnp.float32),
                pltpu.VMEM((UN, E_DEC // 2, 16, 128), jnp.bfloat16),
                pltpu.VMEM((UN, E_DEC, 8, 128), jnp.float32),
                pltpu.VMEM((GB // 8, 8, 8, 128), jnp.float32),
                pltpu.VMEM((128, 128), jnp.bfloat16),
                pltpu.VMEM((E_DEC, GB, 128), jnp.float32)]),
        compiler_params=pltpu.CompilerParams(dimension_semantics=("arbitrary",), vmem_limit_bytes=60 << 20),
        name="dec_attention",
    )((sources * 8).reshape(-1), table, counts.reshape(steps, 1, GB), gs, wq, wo)


def local(
    grid_state,
    hidden_state,
    encoder_sources,
    encoder_counts,
    decoder_sources,
    decoder_counts,
    encoder_keys,
    encoder_values,
    encoder_query,
    encoder_output,
    window_query,
    window_keys,
    window_values,
    window_output,
    feed_up,
    feed_down,
    decoder_query,
    decoder_keys,
    decoder_values,
    decoder_output,
):
    band, head, _, _ = places()
    bands = lax.axis_size("band")
    band_nodes, half_width = hidden_state.shape
    nodes = band_nodes // 2
    grid_count, variables = grid_state.shape
    half_grid = grid_count // 2
    short = 128 - variables
    widen = lambda w: jnp.pad(w, ((0, short), (0, 0)))
    grid = jnp.pad(grid_state, ((0, 0), (0, short)))
    near_grid, state, query, enc_k, enc_v, enc_o, win_q, win_k, win_v, win_o, dec_q, dec_o = start_exchange(
        grid, hidden_state, encoder_query,
        [(widen(encoder_keys), 1), (widen(encoder_values), 1), (encoder_output, 0),
         (window_query, 1), (window_keys, 1), (window_values, 1), (window_output, 0),
         (widen(decoder_query), 1), (jnp.pad(decoder_output, ((0, 0), (0, short))), 0)],
    )
    my_rows = lambda a, size: lax.dynamic_slice_in_dim(a, head * size, size, 0)
    mix = enc_attention(query, enc_k, enc_v, grid, near_grid, my_rows(encoder_sources, nodes), my_rows(encoder_counts, nodes))
    mid = (state.astype(jnp.float32) + jnp.dot(mix, enc_o, preferred_element_type=jnp.float32)).astype(jnp.bfloat16)
    normed = layer_norm(mid)
    span = nodes + 2 * HALF_WIN
    span_rows = nodes - QB + -(-(QB + 2 * HALF_WIN) // 128) * 128
    query, keys, values, up, down = window_span(normed, span_rows, win_q, win_k, win_v, [(feed_up, 1), (feed_down, 0)])
    place = jnp.arange(span_rows, dtype=jnp.int32)
    node = band * band_nodes + head * nodes - HALF_WIN + place
    live = ((place < span) & (node >= 0) & (node < bands * band_nodes))[:, None]
    ones = jnp.broadcast_to(live, (span_rows, 128)).astype(jnp.bfloat16)
    mixed = window(query, keys, values, ones)
    att = (mid.astype(jnp.float32) + jnp.dot(mixed, win_o, preferred_element_type=jnp.float32)).astype(jnp.bfloat16)
    table, hidden_final = final_tables(att, up, down, decoder_keys, decoder_values)
    sources = my_rows(decoder_sources, half_grid) - (band - 1) * band_nodes
    grid_next = decode(table, my_rows(grid, half_grid), dec_q, dec_o, sources,
                       my_rows(decoder_counts, half_grid), variables).T
    return (grid_next, hidden_final)


def solution(mesh):
    in_specs = (
        P("band", None),
        P("band", "head"),
        P("band", None),
        P("band"),
        P("band", None),
        P("band"),
        P(None, "head"),
        P(None, "head"),
        P(None, "head"),
        P("head", None),
        P(None, "head"),
        P(None, "head"),
        P(None, "head"),
        P("head", None),
        P(None, "head"),
        P("head", None),
        P(None, "head"),
        P(None, "head"),
        P(None, "head"),
        P("head", None),
    )
    out_specs = (P(("band", "head"), None), P("band", "head"))
    return jax.shard_map(local, mesh=mesh, in_specs=in_specs, out_specs=out_specs, check_vma=False)
```

```python
import functools

import jax
import jax.numpy as jnp
from jax import lax
from jax.experimental import pallas as pl
from jax.experimental.pallas import tpu as pltpu
from jax.sharding import PartitionSpec as P

HALF_WIN = 560
HEAD_DIM = 64
EPSILON = 1e-05
NEGATIVE = -1e30
SCALE = HEAD_DIM**-0.5
LOG2E = 1.4426950408889634
MESH = pl.DeviceIdType.MESH
NB = 16
QB = 128
GB = 128
UN = 16
ANY = pl.BlockSpec(memory_space=pltpu.HBM)
VM = pl.BlockSpec(memory_space=pltpu.VMEM)


def layer_norm(matrix):
    as_float = matrix.astype(jnp.float32)
    centred = as_float - jnp.mean(as_float, axis=-1, keepdims=True)
    variance = jnp.mean(centred * centred, axis=-1, keepdims=True)
    return (centred * lax.rsqrt(variance + EPSILON)).astype(jnp.bfloat16)


def project(matrix, weight):
    return jnp.dot(matrix, weight, preferred_element_type=jnp.float32).astype(jnp.bfloat16)


def places():
    band = lax.axis_index("band")
    head = lax.axis_index("head")
    count = lax.axis_size("band")
    left = lax.rem(band + count - 1, count)
    right = lax.rem(band + 1, count)
    return band, head, left, right


def greet(others):
    barrier = pltpu.get_barrier_semaphore()
    for other in others:
        pl.semaphore_signal(barrier, inc=1, device_id=other, device_id_type=MESH)
    pl.semaphore_wait(barrier, len(others))


class Sender:
    def __init__(self, send_sem, recv_sem):
        self.send_sem, self.recv_sem, self.used, self.open = send_sem, recv_sem, 0, []

    def send(self, src, dst, device):
        n = self.used
        self.used += 1
        copy = pltpu.make_async_remote_copy(
            src_ref=src, dst_ref=dst, send_sem=self.send_sem.at[n], recv_sem=self.recv_sem.at[n],
            device_id=device, device_id_type=MESH)
        copy.start()
        self.open.append(copy)
        return copy

    def finish(self, received=()):
        for copy in self.open:
            copy.wait_send()
            if not any(copy is other for other in received):
                copy.wait_recv()


def half_of(ref, dim, index):
    size = ref.shape[dim] // 2
    part = pl.ds(pl.multiple_of(index * size, size), size)
    return ref.at[part] if dim == 0 else ref.at[:, part]


def relay(near, source, width, sides, sender, me, band, left, right, head, chunks):
    step = width // 2 // chunks
    waves = []
    for c in range(chunks):
        own = pl.ds(pl.multiple_of(head * (width // 2) + c * step, step), step)
        for side, other in ((sides[0], right), (sides[1], left)):
            rows = pl.ds(pl.multiple_of(side * width + head * (width // 2) + c * step, step), step)
            waves.append((sender.send(source(own, c, step), near.at[rows], (other, head)), rows))
    return waves


def start_kernel(n_pair, dims, *refs):
    grid, state, wq = refs[:3]
    halves = refs[3 : 3 + n_pair]
    near, whole_out, query = refs[3 + n_pair : 6 + n_pair]
    fulls = refs[6 + n_pair : 6 + 2 * n_pair]
    rest = refs[6 + 2 * n_pair :]
    whole, hold_q = rest[:2]
    holds = rest[2 : 2 + n_pair]
    send_sem, recv_sem, load_sem, store_sem = rest[2 + n_pair :]
    band, head, left, right = places()
    peer = (band, 1 - head)
    early = [pltpu.make_async_copy(half_of(state, 0, head), half_of(whole, 1, head), load_sem.at[n_pair]),
             pltpu.make_async_copy(wq, half_of(hold_q, 1, head), load_sem.at[n_pair + 1])]
    loads = [pltpu.make_async_copy(h, v, load_sem.at[n]) for n, (h, v) in enumerate(zip(halves, holds))]
    for load in early + loads:
        load.start()
    greet([peer, (left, head), (right, head)])
    sender = Sender(send_sem, recv_sem)
    waves = relay(near, lambda own, c, step: grid.at[own], grid.shape[0], (0, 1), sender, None, band, left, right, head, 4)
    first = [sender.send(half_of(state, 0, 1 - head), half_of(whole, 1, head), peer),
             sender.send(wq, half_of(hold_q, 1, head), peer)]
    for n in range(n_pair):
        sender.send(halves[n], half_of(fulls[n], dims[n], head), peer)
    stores = [pltpu.make_async_copy(holds[n], half_of(fulls[n], dims[n], head), store_sem.at[n]) for n in range(n_pair)]
    for load, store in zip(loads, stores):
        load.wait()
        store.start()
    for load in early:
        load.wait()
    for copy in first:
        copy.wait_recv()
    block = whole.shape[0] // 2
    for b in range(2):
        x = whole[b * block:(b + 1) * block, :]
        whole_out[b * block:(b + 1) * block, :] = x
        query[b * block:(b + 1) * block, :] = project(layer_norm(x), hold_q[...])
    for copy, rows in waves:
        copy.wait_recv()
        sender.send(near.at[rows], near.at[rows], peer)
    sender.finish([copy for copy, _ in waves] + first)
    for store in stores:
        store.wait()


def full_shape(half, dim):
    shape = list(half.shape)
    shape[dim] *= 2
    return jax.ShapeDtypeStruct(tuple(shape), half.dtype)


def start_exchange(grid, state, wq, pairs):
    halves = [half for half, _ in pairs]
    dims = [dim for _, dim in pairs]
    n = len(pairs)
    nodes, width = state.shape
    rows = jax.ShapeDtypeStruct((nodes // 2, width * 2), state.dtype)
    outs = [jax.ShapeDtypeStruct((2 * grid.shape[0], grid.shape[1]), grid.dtype), rows, rows]
    outs += [full_shape(half, dim) for half, dim in pairs]
    copies = 16 + 2 + n
    return pl.pallas_call(
        functools.partial(start_kernel, n, dims),
        out_shape=outs,
        in_specs=[VM] + [ANY] * (n + 2),
        out_specs=[ANY, VM, VM] + [ANY] * n,
        scratch_shapes=[pltpu.VMEM(rows.shape, state.dtype), pltpu.VMEM(full_shape(wq, 1).shape, wq.dtype)]
        + [pltpu.VMEM(half.shape, half.dtype) for half in halves]
        + [pltpu.SemaphoreType.DMA((copies,))] * 2
        + [pltpu.SemaphoreType.DMA((n + 2,)), pltpu.SemaphoreType.DMA((n,))],
        compiler_params=pltpu.CompilerParams(collective_id=0, has_side_effects=True, vmem_limit_bytes=60 << 20),
        name="start_exchange",
    )(grid, state, wq, *halves)


def span_kernel(n_pair, dims, *refs):
    rows, wq, wk, wv = refs[:4]
    halves = refs[4 : 4 + n_pair]
    q, k, v = refs[4 + n_pair : 7 + n_pair]
    fulls = refs[7 + n_pair : 7 + 2 * n_pair]
    span, hold_q, hold_k, hold_v = refs[7 + 2 * n_pair : 11 + 2 * n_pair]
    holds = refs[11 + 2 * n_pair : 11 + 3 * n_pair]
    send_sem, recv_sem, load_sem, store_sem = refs[11 + 3 * n_pair :]
    band, head, left, right = places()
    bands = lax.axis_size("band")
    count, width = rows.shape
    extra = HALF_WIN - count
    after = HALF_WIN + count
    chunks = 4
    step = count // chunks
    peer = (band, 1 - head)
    beside = (lax.rem(band + bands + 2 * head - 1, bands), 1 - head)
    weights = [pltpu.make_async_copy(w, hold, load_sem.at[n_pair + n]) for n, (w, hold) in enumerate(((wq, hold_q), (wk, hold_k), (wv, hold_v)))]
    for load in weights:
        load.start()
    loads = [pltpu.make_async_copy(h, hold, load_sem.at[n]) for n, (h, hold) in enumerate(zip(halves, holds))]
    for load in loads:
        load.start()
    greet([peer, (left, head), (right, head), beside])
    sender = Sender(send_sem, recv_sem)
    from_beside = extra + head * (after - extra)
    from_peer = after + head * (extra - after)
    first = sender.send(rows.at[pl.ds(count - extra, extra)], span.at[pl.ds(0, extra)], (right, head))
    last = sender.send(rows.at[pl.ds(0, extra)], span.at[pl.ds(after + count, extra)], (left, head))
    waves = [sender.send(rows.at[pl.ds(c * step, step)], span.at[pl.ds(pl.multiple_of(from_peer + c * step, 16), step)], beside)
             for c in range(chunks)]
    partner = sender.send(rows, span.at[pl.ds(pl.multiple_of(from_beside, 16), count)], peer)
    for n in range(n_pair):
        sender.send(halves[n], half_of(fulls[n], dims[n], head), peer)
    for load in weights:
        load.wait()

    def pair(x, place, size):
        node = band * (2 * count) + head * count - HALF_WIN + place + lax.broadcasted_iota(jnp.int32, (size, 1), 0)
        live = (node >= 0) & (node < bands * 2 * count)
        for w, o in ((hold_k, k), (hold_v, v)):
            o[pl.ds(place, size), :] = jnp.where(live, jnp.dot(x, w[...], preferred_element_type=jnp.float32), 0.0).astype(jnp.bfloat16)

    half = count // 2
    for b in range(2):
        x = rows[b * half:(b + 1) * half, :]
        q[b * half:(b + 1) * half, :] = jnp.dot(x, hold_q[...], preferred_element_type=jnp.float32).astype(jnp.bfloat16)
        pair(x, HALF_WIN + b * half, half)
    stores = [pltpu.make_async_copy(holds[n], half_of(fulls[n], dims[n], head), store_sem.at[n]) for n in range(n_pair)]
    for load, store in zip(loads, stores):
        load.wait()
        store.start()
    partner.wait_recv()
    for b in range(2):
        place = pl.multiple_of(from_peer + b * half, 16)
        pair(span[pl.ds(place, half), :], place, half)
    first.wait_recv()
    last.wait_recv()
    tail = span.shape[0] - after - count - extra
    pad = jnp.zeros((tail, width), rows.dtype)
    pair(span[0:extra, :], 0, extra)
    pair(jnp.concatenate((span[after + count:after + count + extra, :], pad), axis=0), after + count, extra + tail)
    for b in range(2):
        for c in range(b * chunks // 2, (b + 1) * chunks // 2):
            waves[c].wait_recv()
        place = pl.multiple_of(from_beside + b * half, 16)
        pair(span[pl.ds(place, half), :], place, half)
    sender.finish(waves + [first, last, partner])
    for store in stores:
        store.wait()


def window_span(rows, span_rows, wq, wk, wv, pairs):
    halves = [half for half, _ in pairs]
    dims = [dim for _, dim in pairs]
    n = len(pairs)
    outs = [jax.ShapeDtypeStruct((size, rows.shape[1]), rows.dtype) for size in (rows.shape[0], span_rows, span_rows)]
    outs += [full_shape(half, dim) for half, dim in pairs]
    copies = 7 + n
    return pl.pallas_call(
        functools.partial(span_kernel, n, dims),
        out_shape=outs,
        in_specs=[VM] + [ANY] * (n + 3),
        out_specs=[VM] * 3 + [ANY] * n,
        scratch_shapes=[pltpu.VMEM((span_rows, rows.shape[1]), rows.dtype)]
        + [pltpu.VMEM(w.shape, w.dtype) for w in (wq, wk, wv)]
        + [pltpu.VMEM(half.shape, half.dtype) for half in halves]
        + [pltpu.SemaphoreType.DMA((copies,))] * 2
        + [pltpu.SemaphoreType.DMA((n + 3,)), pltpu.SemaphoreType.DMA((n,))],
        compiler_params=pltpu.CompilerParams(collective_id=1, has_side_effects=True, vmem_limit_bytes=46 << 20),
        name="window_span",
    )(rows, wq, wk, wv, *halves)


def tables_kernel(att, up, down, wk, wv, table, out, rows, inner, near, hold_u, hold_d, hold_k, hold_v, blocks,
                  send_sem, recv_sem, load_sem, store_sem):
    band, head, left, right = places()
    count, width = rows.shape
    chunks = 4
    step = count // chunks
    block = count // 2
    peer = (band, 1 - head)
    lines = blocks.reshape(blocks.shape[0] * blocks.shape[1] * blocks.shape[2] * 8, 128)
    feeds = [pltpu.make_async_copy(up, hold_u, load_sem.at[2]), pltpu.make_async_copy(down, hold_d, load_sem.at[3])]
    loads = [pltpu.make_async_copy(half, half_of(hold, 1, head), load_sem.at[n])
             for n, (half, hold) in enumerate(((wk, hold_k), (wv, hold_v)))]
    for load in feeds + loads:
        load.start()
    greet([peer, (left, head), (right, head)])

    def side_rows(side, c):
        return pl.ds(pl.multiple_of(side * count + head * count + c * step, step), step)

    def across(c, side):
        return pltpu.make_async_remote_copy(
            src_ref=rows.at[pl.ds(pl.multiple_of(c * step, step), step)], dst_ref=near.at[side_rows(side, c)],
            send_sem=send_sem.at[2 * c + side // 4], recv_sem=recv_sem.at[2 * c + side // 4],
            device_id=(left if side else right, head), device_id_type=MESH)

    def passed(c, side):
        ours = near.at[side_rows(side, c)]
        n = 2 * c + side // 4 + 2 * chunks
        return pltpu.make_async_remote_copy(
            src_ref=ours, dst_ref=ours, send_sem=send_sem.at[n], recv_sem=recv_sem.at[n],
            device_id=peer, device_id_type=MESH)

    base = 2 * count + head * count
    mine = [pl.ds(pl.multiple_of(base + h * block, block), block) for h in range(2)]
    local = [pltpu.make_async_remote_copy(
        src_ref=src, dst_ref=dst, send_sem=send_sem.at[4 * chunks + n], recv_sem=recv_sem.at[4 * chunks + n],
        device_id=peer, device_id_type=MESH)
        for n, (src, dst) in enumerate(((wk, half_of(hold_k, 1, head)), (wv, half_of(hold_v, 1, head)),
                                        (rows.at[0:block], near.at[mine[0]]), (rows.at[block:], near.at[mine[1]])))]
    for copy in local[:2]:
        copy.start()

    def send_half(h):
        for c in range(h * chunks // 2, (h + 1) * chunks // 2):
            for side in (0, 4):
                across(c, side).start()
        local[2 + h].start()

    feeds[0].wait()
    part = up.shape[1] // 8
    for h in range(2):
        x = att[h * block:(h + 1) * block, :]
        xn = layer_norm(x)
        if h == 1:
            send_half(0)

        def rise(n, carry):
            for m in range(2):
                cols = pl.ds(pl.multiple_of((2 * n + m) * part, part), part)
                up_rows = jnp.dot(xn, hold_u[:, cols], preferred_element_type=jnp.float32)
                inner[:, cols] = jax.nn.gelu(up_rows, approximate=True).astype(jnp.bfloat16)
            return carry

        lax.fori_loop(0, 4, rise, 0)
        if h == 0:
            feeds[1].wait()
        for n in range(2):
            cols = slice(n * width // 2, (n + 1) * width // 2)
            total = x[:, cols].astype(jnp.float32) + jnp.dot(inner[...], hold_d[:, cols], preferred_element_type=jnp.float32)
            total = total.astype(jnp.bfloat16)
            rows[h * block:(h + 1) * block, cols] = total
            near[mine[h], cols] = total

    def stores(base, slot):
        return [pltpu.make_async_copy(
            blocks.at[slot, kind, pl.ds(half * step, step)],
            table.at[pl.ds(pl.multiple_of(kind * (6 * count) + base + half * count, step), step)],
            store_sem.at[slot, 2 * kind + half]) for kind in range(2) for half in range(2)]

    def project_block(base, turn):
        slot = lax.rem(turn, 2)

        @pl.when(turn >= 2)
        def _():
            for store in stores(base, slot):
                store.wait()

        pieces = [pl.multiple_of(base + part * count, step) for part in range(2)]
        xf = jnp.concatenate([near[pl.ds(p, step), :] for p in pieces], axis=0).astype(jnp.float32)
        cen = xf - jnp.mean(xf, axis=-1, keepdims=True)
        var = jnp.mean(cen * cen, axis=-1, keepdims=True)
        xn = (cen * lax.rsqrt(var + EPSILON)).astype(jnp.bfloat16)
        for part, w in enumerate((hold_k, hold_k, hold_v, hold_v)):
            kv = jnp.dot(xn, w[:, part % 2 * 512:part % 2 * 512 + 512], preferred_element_type=jnp.float32)
            for s in range(4):
                at = part // 2 * (2 * step * 8) + part % 2 * 4 + s
                lines[pl.ds(slot * (4 * step * 8) + at, 2 * step, stride=8), :] = kv[:, s * 128:(s + 1) * 128]
        for store in stores(base, slot):
            store.start()

    for load in loads:
        load.wait()
    for copy in local[:2]:
        copy.wait_recv()

    def own(c, turn):
        project_block(2 * count + c * step, turn)
        return turn + 1

    def waves(c, turn):
        for side in (0, 4):
            across(c, side).wait_recv()
            passed(c, side).start()
        for side in (0, 4):
            passed(c, side).wait_recv()
            project_block(side * count + c * step, turn + side // 4)
        return turn + 2

    local[2].wait_recv()
    turn = lax.fori_loop(0, 2, own, 0)
    send_half(1)
    turn = lax.fori_loop(0, 2, waves, turn)
    local[3].wait_recv()
    turn = lax.fori_loop(2, 4, own, turn)
    out[...] = near[2 * count:4 * count, pl.ds(pl.multiple_of(head * (width // 2), width // 2), width // 2)]
    lax.fori_loop(2, 4, waves, turn)
    for slot in range(2):
        for store in stores(0, slot):
            store.wait()
    for c in range(chunks):
        for side in (0, 4):
            across(c, side).wait_send()
            passed(c, side).wait_send()
    for copy in local:
        copy.wait_send()


def final_tables(att, up, down, wk, wv):
    count, width = att.shape
    whole = (wk.shape[0], 2 * wk.shape[1])
    return pl.pallas_call(
        tables_kernel,
        out_shape=[jax.ShapeDtypeStruct((12 * count, 8, 128), jnp.float32), jax.ShapeDtypeStruct((2 * count, width // 2), att.dtype)],
        in_specs=[VM, ANY, ANY, ANY, ANY],
        out_specs=[ANY, VM],
        scratch_shapes=[
            pltpu.VMEM((count, width), att.dtype),
            pltpu.VMEM((count // 2, up.shape[1]), att.dtype),
            pltpu.VMEM((6 * count, width), att.dtype),
            pltpu.VMEM(up.shape, up.dtype),
            pltpu.VMEM(down.shape, down.dtype),
            pltpu.VMEM(whole, wk.dtype),
            pltpu.VMEM(whole, wv.dtype),
            pltpu.VMEM((2, 2, count // 2, 8, 128), jnp.float32),
            pltpu.SemaphoreType.DMA((20,)),
            pltpu.SemaphoreType.DMA((20,)),
            pltpu.SemaphoreType.DMA((4,)),
            pltpu.SemaphoreType.DMA((2, 4))],
        compiler_params=pltpu.CompilerParams(collective_id=2, has_side_effects=True, vmem_limit_bytes=60 << 20),
        name="final_tables",
    )(att, up, down, wk, wv)


E_ENC = 32
E_DEC = 4


def enc_kernel(idx, q, wk, wv, go, near, bias, out, table, g_a, g_b, qk, mg, wk_pad, wv_pad):
    i = pl.program_id(0)
    steps = pl.num_programs(0)
    nodes = q.shape[0]
    heads2 = q.shape[1] // 128
    lane = lax.broadcasted_iota(jnp.int32, (1, 128), 1)
    low = lane < 64

    @pl.when(i == 0)
    def _():
        band = go.shape[0]
        for part, ref in enumerate((near.at[0:band], go, near.at[band:])):
            @pl.loop(0, band // 128)
            def _(b):
                r = pl.multiple_of(b * 128, 128)
                table[pl.ds(part * band + r, 128), :] = ref[pl.ds(r, 128), :].astype(jnp.float32)
        for pad, small in ((wk_pad, wk), (wv_pad, wv)):
            pad[...] = jnp.zeros_like(pad)
            pad[0:small.shape[0], :] = small[...]
        for c in range(heads2):
            qc = q[:, c * 128:(c + 1) * 128].astype(jnp.float32)
            wc = wk_pad[:, c * 128:(c + 1) * 128]
            for par in range(2):
                qm = jnp.where(low if par == 0 else ~low, qc, 0.0).astype(jnp.bfloat16)
                r = lax.dot_general(qm, wc, (((1,), (1,)), ((), ())), preferred_element_type=jnp.float32)
                qk[2 * c + par] = (r * SCALE).astype(jnp.bfloat16)

    rows = NB * E_ENC

    def gather(block, g):
        base = block * rows
        for r in range(rows):
            g[r:r + 1, :] = table[pl.ds(idx[base + r], 1), :]

    def mixing(block, g):
        gb = g[...].astype(jnp.bfloat16)
        n0 = pl.multiple_of(block * NB, NB)
        qb = qk[:, pl.ds(n0, NB), :].reshape(heads2 * 2 * NB, 128)
        s = lax.dot_general(qb, gb, (((1,), (1,)), ((), ())), preferred_element_type=jnp.float32)
        rn = lax.broadcasted_iota(jnp.int32, s.shape, 0) % NB
        cn = lax.broadcasted_iota(jnp.int32, s.shape, 1) // E_ENC
        s = jnp.where(rn == cn, s + bias[block], NEGATIVE)
        p = jnp.exp(s)
        l = jnp.sum(p, axis=-1, keepdims=True)
        m = jnp.dot(p.astype(jnp.bfloat16), gb, preferred_element_type=jnp.float32) / l
        mg[:, pl.ds(n0, NB), :] = m.astype(jnp.bfloat16).reshape(heads2 * 2, NB, 128)

    gather(2 * i, g_a)
    mixing(jnp.maximum(2 * i - 1, 0), g_b)
    gather(2 * i + 1, g_b)
    mixing(2 * i, g_a)

    @pl.when(i == steps - 1)
    def _():
        mixing(2 * i + 1, g_b)
        for c in range(heads2):
            wc = wv_pad[:, c * 128:(c + 1) * 128]
            a = jnp.dot(mg[2 * c], wc, preferred_element_type=jnp.float32)
            b = jnp.dot(mg[2 * c + 1], wc, preferred_element_type=jnp.float32)
            out[:, c * 128:(c + 1) * 128] = jnp.where(low, a, b).astype(jnp.bfloat16)

def enc_attention(q, wk, wv, go, near, sources, counts):
    nodes, width = q.shape
    slots = sources.shape[1]
    steps = nodes // NB
    live = jnp.arange(slots, dtype=jnp.int32)[None, :] < counts[:, None]
    bias = jnp.where(live, 0.0, NEGATIVE).astype(jnp.float32).reshape(steps, 1, NB * slots)
    full = lambda a: pl.BlockSpec(a.shape, lambda i, s: (0,) * a.ndim, pipeline_mode=pl.Buffered(1))
    return pl.pallas_call(
        enc_kernel,
        out_shape=jax.ShapeDtypeStruct((nodes, width), jnp.bfloat16),
        grid_spec=pltpu.PrefetchScalarGridSpec(
            num_scalar_prefetch=1, grid=(steps // 2,),
            in_specs=[full(q), full(wk), full(wv), full(go), full(near),
                      full(bias)],
            out_specs=pl.BlockSpec((nodes, width), lambda i, s: (0, 0)),
            scratch_shapes=[
                pltpu.VMEM((3 * go.shape[0], 128), jnp.float32),
                pltpu.VMEM((NB * slots, 128), jnp.float32),
                pltpu.VMEM((NB * slots, 128), jnp.float32),
                pltpu.VMEM((width // 64, nodes, 128), jnp.bfloat16),
                pltpu.VMEM((width // 64, nodes, 128), jnp.bfloat16),
                pltpu.VMEM((128, width), jnp.bfloat16),
                pltpu.VMEM((128, width), jnp.bfloat16)]),
        compiler_params=pltpu.CompilerParams(dimension_semantics=("arbitrary",), vmem_limit_bytes=48 << 20),
        cost_estimate=pl.CostEstimate(flops=4 << 30, bytes_accessed=8 << 20, transcendentals=4 << 20),
        name="enc_attention",
    )(sources.reshape(-1), q, wk, wv, go, near, bias)


def win_kernel(q, k, v, ones, out, p):
    nodes = q.shape[0]
    span = p.shape[-1]
    lane = lax.broadcasted_iota(jnp.int32, (1, 128), 1)
    low = lane < 64
    for b in range(nodes // QB):
        s0 = b * QB
        kb = k[s0:s0 + span, :]
        ve = jnp.concatenate((v[s0:s0 + span, :], ones[s0:s0 + span, :]), axis=1)
        qc = q[s0:s0 + QB, :].astype(jnp.float32) * SCALE
        res = []
        for par in range(2):
            qm = jnp.where(low if par == 0 else ~low, qc, 0.0).astype(jnp.bfloat16)
            for t in range(0, span, 256):
                w = min(256, span - t)
                s = lax.dot_general(qm, kb[t:t + w, :], (((1,), (1,)), ((), ())), preferred_element_type=jnp.float32)
                e = jnp.exp(s)
                if t < QB or t + w - 1 > 2 * HALF_WIN:
                    d = lax.broadcasted_iota(jnp.int32, s.shape, 1) + t - lax.broadcasted_iota(jnp.int32, s.shape, 0)
                    e = jnp.where((d >= 0) & (d <= 2 * HALF_WIN), e, 0.0)
                p[2*b+par, :, t:t + w] = e.astype(jnp.bfloat16)
            o = jnp.dot(p[2*b+par], ve, preferred_element_type=jnp.float32)
            res.append(o[:, :128] / o[:, 128:])
        out[s0:s0 + QB, :] = jnp.where(low, res[0], res[1]).astype(jnp.bfloat16)

def window(q, k, v, ones):
    nodes, width = q.shape
    span = -(-(QB + 2 * HALF_WIN) // 128) * 128
    keys = k.shape[0]
    return pl.pallas_call(
        win_kernel, out_shape=jax.ShapeDtypeStruct((nodes, width), jnp.bfloat16),
        grid=(width // 128,),
        in_specs=[pl.BlockSpec((nodes, 128), lambda c: (0, c)), pl.BlockSpec((keys, 128), lambda c: (0, c)),
                  pl.BlockSpec((keys, 128), lambda c: (0, c)), pl.BlockSpec((keys, 128), lambda c: (0, 0))],
        out_specs=pl.BlockSpec((nodes, 128), lambda c: (0, c)),
        scratch_shapes=[pltpu.VMEM((2*nodes//QB, QB, span), jnp.bfloat16)],
        compiler_params=pltpu.CompilerParams(dimension_semantics=("arbitrary",), vmem_limit_bytes=48 << 20),
        name="window_attention")(q, k, v, ones)


def dec_kernel(idx, table, cnt, gs, wq, wo, out, q3, prod_a, held_a, prod_b, held_b, mix3, seg, live, wq_pad):
    i = pl.program_id(0)
    rows = table.shape[0] // 2
    lines = table.reshape(table.shape[0] * 8, 128)
    qlines = q3.reshape(GB * 8, 128)
    lives = live.reshape(E_DEC * GB, 128)
    mlines = mix3.reshape(GB * 8, 128)
    lane = lax.broadcasted_iota(jnp.int32, (1, 128), 1)

    @pl.when(i == 0)
    def _():
        r = lax.broadcasted_iota(jnp.int32, (128, 128), 0) // 64
        c = lax.broadcasted_iota(jnp.int32, (128, 128), 1) // 64
        seg[...] = jnp.where(r == c, 1.0, 0.0).astype(jnp.bfloat16)
        wq_pad[...] = jnp.zeros_like(wq_pad)
        wq_pad[0:wq.shape[0], :] = wq[...]

    def work():
        g0 = i * GB
        gb = gs[...]
        qf = jnp.dot(gb, wq_pad[...], preferred_element_type=jnp.float32) * (SCALE * LOG2E)
        for s in range(8):
            q3[:, s] = qf[:, s * 128:(s + 1) * 128].reshape(GB // 8, 8, 128)
        slots = jnp.broadcast_to(cnt[0].astype(jnp.float32), (128, GB)).T
        for e in range(E_DEC):
            live[e] = jnp.where(slots > e, 1.0, 0.0)

        def gather(o, prod, held):
            base = (g0 + o * UN) * E_DEC
            for j in range(UN):
                place = (j // 8) * 64 + j % 8
                qv = qlines[pl.ds(pl.multiple_of(o * (UN * 8), 64) + place, 8, stride=8), :]
                parts = []
                for e in range(E_DEC):
                    at = pl.multiple_of(idx[base + (j * E_DEC + e)], 8)
                    parts.append(qv * lines[pl.ds(at, 8), :])
                    held[j, e] = lines[pl.ds(at + rows * 8, 8), :]
                for h in range(E_DEC // 2):
                    prod[j, h] = jnp.concatenate(parts[2 * h:2 * h + 2], axis=0).astype(jnp.bfloat16)

        def mixing(o, prod, held):
            pm = prod[...].reshape(E_DEC * UN * 8, 128)
            sc = jnp.dot(pm, seg[...], preferred_element_type=jnp.float32).reshape(UN, E_DEC, 8, 128)
            for j in range(UN):
                tot = None
                for e in range(E_DEC):
                    pe = jnp.exp2(sc[j, e])
                    if e > 0:
                        pe = pe * lives[pl.ds(e * GB + (o * UN + j), 8, stride=0), :]
                    pv = pe * held[j, e]
                    tot = pe if e == 0 else tot + pe
                    acc = pv if e == 0 else acc + pv
                place = (j // 8) * 64 + j % 8
                mlines[pl.ds(pl.multiple_of(o * (UN * 8), 64) + place, 8, stride=8), :] = acc / tot

        rounds = GB // UN
        gather(0, prod_a, held_a)

        def both(o, carry):
            gather(2 * o + 1, prod_b, held_b)
            mixing(2 * o, prod_a, held_a)
            gather(2 * o + 2, prod_a, held_a)
            mixing(2 * o + 1, prod_b, held_b)
            return carry

        lax.fori_loop(0, rounds // 2 - 1, both, 0)
        gather(rounds - 1, prod_b, held_b)
        mixing(rounds - 2, prod_a, held_a)
        mixing(rounds - 1, prod_b, held_b)
        m2 = jnp.concatenate([mix3[:, s].reshape(GB, 128) for s in range(8)], axis=1).astype(jnp.bfloat16)
        update = lax.dot_general(wo[...], m2, (((1,), (1,)), ((), ())), preferred_element_type=jnp.float32)
        old = gb.astype(jnp.float32).T[:out.shape[0], :]
        out[...] = (old + update).astype(jnp.bfloat16)

    work()

def decode(table, gs, wq, wo, sources, counts, variables):
    grid_rows = gs.shape[0]
    steps = grid_rows // GB
    full = lambda a: pl.BlockSpec(a.shape, lambda i, *_: (0,) * a.ndim, pipeline_mode=pl.Buffered(1))
    late = lambda i, *_: (i, 0)
    return pl.pallas_call(
        dec_kernel,
        out_shape=jax.ShapeDtypeStruct((variables, grid_rows), jnp.bfloat16),
        grid_spec=pltpu.PrefetchScalarGridSpec(
            num_scalar_prefetch=1, grid=(steps,),
            in_specs=[full(table),
                      pl.BlockSpec((1, 1, GB), lambda i, *_: (i, 0, 0)), pl.BlockSpec((GB, 128), late), full(wq), full(wo)],
            out_specs=pl.BlockSpec((variables, GB), lambda i, *_: (0, i)),
            scratch_shapes=[
                pltpu.VMEM((GB // 8, 8, 8, 128), jnp.float32),
                pltpu.VMEM((UN, E_DEC // 2, 16, 128), jnp.bfloat16),
                pltpu.VMEM((UN, E_DEC, 8, 128), jnp.float32),
                pltpu.VMEM((UN, E_DEC // 2, 16, 128), jnp.bfloat16),
                pltpu.VMEM((UN, E_DEC, 8, 128), jnp.float32),
                pltpu.VMEM((GB // 8, 8, 8, 128), jnp.float32),
                pltpu.VMEM((128, 128), jnp.bfloat16),
                pltpu.VMEM((E_DEC, GB, 128), jnp.float32),
                pltpu.VMEM((128, wq.shape[1]), jnp.bfloat16)]),
        compiler_params=pltpu.CompilerParams(dimension_semantics=("arbitrary",), vmem_limit_bytes=60 << 20),
        name="dec_attention",
    )((sources * 8).reshape(-1), table, counts.reshape(steps, 1, GB), gs, wq, wo)


def local(
    grid_state,
    hidden_state,
    encoder_sources,
    encoder_counts,
    decoder_sources,
    decoder_counts,
    encoder_keys,
    encoder_values,
    encoder_query,
    encoder_output,
    window_query,
    window_keys,
    window_values,
    window_output,
    feed_up,
    feed_down,
    decoder_query,
    decoder_keys,
    decoder_values,
    decoder_output,
):
    band, head, _, _ = places()
    bands = lax.axis_size("band")
    band_nodes, half_width = hidden_state.shape
    nodes = band_nodes // 2
    grid_count, variables = grid_state.shape
    half_grid = grid_count // 2
    short = 128 - variables
    grid = jnp.pad(grid_state, ((0, 0), (0, short)))
    near_grid, state, query, enc_k, enc_v, enc_o, win_q, win_k, win_v, win_o, dec_q, dec_o = start_exchange(
        grid, hidden_state, encoder_query,
        [(encoder_keys, 1), (encoder_values, 1), (encoder_output, 0),
         (window_query, 1), (window_keys, 1), (window_values, 1), (window_output, 0),
         (decoder_query, 1), (decoder_output.T, 1)],
    )
    my_rows = lambda a, size: lax.dynamic_slice_in_dim(a, head * size, size, 0)
    mix = enc_attention(query, enc_k, enc_v, grid, near_grid, my_rows(encoder_sources, nodes), my_rows(encoder_counts, nodes))
    mid = (state.astype(jnp.float32) + jnp.dot(mix, enc_o, preferred_element_type=jnp.float32)).astype(jnp.bfloat16)
    normed = layer_norm(mid)
    span = nodes + 2 * HALF_WIN
    span_rows = nodes - QB + -(-(QB + 2 * HALF_WIN) // 128) * 128
    query, keys, values, up, down = window_span(normed, span_rows, win_q, win_k, win_v, [(feed_up, 1), (feed_down, 0)])
    place = jnp.arange(span_rows, dtype=jnp.int32)
    node = band * band_nodes + head * nodes - HALF_WIN + place
    live = ((place < span) & (node >= 0) & (node < bands * band_nodes))[:, None]
    ones = jnp.broadcast_to(live, (span_rows, 128)).astype(jnp.bfloat16)
    mixed = window(query, keys, values, ones)
    att = (mid.astype(jnp.float32) + jnp.dot(mixed, win_o, preferred_element_type=jnp.float32)).astype(jnp.bfloat16)
    table, hidden_final = final_tables(att, up, down, decoder_keys, decoder_values)
    sources = my_rows(decoder_sources, half_grid) - (band - 1) * band_nodes
    grid_next = decode(table, my_rows(grid, half_grid), dec_q, dec_o, sources,
                       my_rows(decoder_counts, half_grid), variables).T
    return (grid_next, hidden_final)


def solution(mesh):
    in_specs = (
        P("band", None),
        P("band", "head"),
        P("band", None),
        P("band"),
        P("band", None),
        P("band"),
        P(None, "head"),
        P(None, "head"),
        P(None, "head"),
        P("head", None),
        P(None, "head"),
        P(None, "head"),
        P(None, "head"),
        P("head", None),
        P(None, "head"),
        P("head", None),
        P(None, "head"),
        P(None, "head"),
        P(None, "head"),
        P("head", None),
    )
    out_specs = (P(("band", "head"), None), P("band", "head"))
    return jax.shard_map(local, mesh=mesh, in_specs=in_specs, out_specs=out_specs, check_vma=False)
```
